32 devices in a mesh: gx: 4 (over z), gy: 2 (over x), gz: 4 (over y, core).
Axes of the slice: x: 2, y: 2, z: 4, core: 2. Of those that a mesh axis runs over, the one named last changes fastest.
Arguments:
- volume: bfloat16 [64, 256, 512], P('gz', 'gy', 'gx'), may hold values from 0 to 1
- hat_center: int32 [256], replicated, may hold values from 0 to 255
- tf_table: bfloat16 [4, 256], replicated, may hold values from 0.049804688 to 1
Outputs:
- image: float32 [4, 256, 512], P(None, 'gy')
The draws below stay inside these ranges and needn't reach their ends.
All inputs are finite; a program needn't handle non-finite values.
Results may differ from the reference program's by a relative error of at most 0.0003.
Values may be sent and summed in bfloat16 or wider, within the bound.
A program may use at most 64 MiB of HBM per device.

```python
import math
import jax
import jax.numpy as jnp
from jax import lax

NBIN = 256
HW = 4
NX = 512
NY = 256
NZ = 64


def set_ends(values, stream_key, low, top_value):
    longest = values.shape.index(max(values.shape))
    spots = []
    for shift in (0, 1):
        where = [jax.random.randint(jax.random.fold_in(stream_key, axis), (), 0, length) for axis, length in enumerate(values.shape)]
        where[longest] = (where[longest] + shift) % values.shape[longest]
        spots.append(tuple(where))
    return values.at[spots[0]].set(low).at[spots[1]].set(top_value)


def block_levels(own_key, dims, split, smallest, top_value):
    def one(dim, blocks):
        steps = jax.random.uniform(jax.random.fold_in(jax.random.fold_in(own_key, 6), dim), (blocks,), jnp.float32, smallest / len(split), top_value / len(split))
        return jnp.repeat(jnp.exp(steps), dims[dim] // blocks).reshape((-1,) + (1,) * (len(dims) - dim - 1))

    factor_of = one(*split[0])
    for cut in split[1:]:
        factor_of = factor_of * one(*cut)
    return factor_of


def setup_inputs(seed: int = 0) -> dict:
    splits = jax.random.split(jax.random.key(seed), 4)
    volume = jnp.clip(1.0 * jax.random.uniform(splits[0], (NZ, NY, NX), jnp.float32) ** block_levels(splits[0], (NZ, NY, NX), ((0, 4), (1, 2), (2, 4)), -0.2, 0.2), 0.0, 1.0).astype(jnp.bfloat16)
    hat_center = set_ends(jax.random.randint(splits[1], (NBIN,), 0, NBIN), jax.random.fold_in(splits[1], 1), 0, NBIN - 1).astype(jnp.int32)
    tf_table = jnp.clip(jnp.exp(jax.random.uniform(splits[2], (4, NBIN), jnp.float32, math.log(0.049804688), math.log(1.0))), 0.049804688, 1.0).astype(jnp.bfloat16)
    return dict(volume=volume, hat_center=hat_center, tf_table=tf_table)


ambient = 0.3
grad_floor = 0.01
depth_scale = 1.5

def smooth(values, along):
    length = values.shape[along] - 2
    return lax.slice_in_dim(values, 0, length, axis=along) + 2.0 * lax.slice_in_dim(values, 1, length + 1, axis=along) + lax.slice_in_dim(values, 2, length + 2, axis=along)

def differ(values, along):
    length = values.shape[along] - 2
    return lax.slice_in_dim(values, 2, length + 2, axis=along) - lax.slice_in_dim(values, 0, length, axis=along)

def shading(padded):
    grad_x = smooth(smooth(differ(padded, 2), 1), 0) / 32.0
    grad_y = smooth(smooth(differ(padded, 1), 2), 0) / 32.0
    grad_z = smooth(smooth(differ(padded, 0), 2), 1) / 32.0
    facing = jnp.abs(grad_x + grad_y + grad_z) / jnp.sqrt(3.0)
    length = jnp.sqrt(grad_x * grad_x + grad_y * grad_y + grad_z * grad_z + grad_floor)
    return ambient + (1.0 - ambient) * facing / length

def colour(voxels, centers, tf_table):
    bin_level = voxels.astype(jnp.float32) * (NBIN - 1)
    hat_values = jnp.maximum(0.0, 1.0 - jnp.abs(bin_level[None, :] - centers[:, None]) / HW).astype(jnp.bfloat16)
    return jnp.dot(tf_table, hat_values, preferred_element_type=jnp.float32)

def reference(volume, hat_center, tf_table):
    planes, height, across = volume.shape
    centers = hat_center.astype(jnp.float32)
    transfer = lax.map(lambda slab_plane: colour(slab_plane.reshape(-1), centers, tf_table), volume)
    transfer = transfer.reshape(planes, 4, height, across)
    shading_term = shading(jnp.pad(volume.astype(jnp.float32), 1))
    opacity = 1.0 - jnp.exp(-transfer[:, 3] * (depth_scale / planes))
    emitted = transfer[:, :3] * shading_term[:, None]
    through = jnp.cumprod(1.0 - opacity, axis=0)
    before = jnp.concatenate([jnp.ones_like(through[:1]), through[:-1]], axis=0)
    colour_sum = lax.optimization_barrier(jnp.sum((before * opacity)[:, None] * emitted, axis=0))
    return jnp.concatenate([colour_sum, 1.0 - through[-1][None]], axis=0)
```

```python
import functools

import jax
import jax.numpy as jnp
from jax import lax
from jax.experimental import pallas as pl
from jax.experimental.pallas import tpu as pltpu
from jax.sharding import PartitionSpec as P

NBIN = 256
HW = 4

ambient = 0.3
grad_floor = 0.01
depth_scale = 1.5

LANES = 128
BINADES = 8
GROUPS = BINADES + 5
MESH = pl.DeviceIdType.MESH
F32 = jnp.float32
BF16 = jnp.bfloat16


def build_tables(center_ref, table_ref, tab):
    centers = center_ref[...].astype(F32)
    wide = table_ref[...].astype(F32)
    copies = jnp.concatenate(
        [jnp.broadcast_to(wide[c : c + 1], (8, NBIN)) for c in range(4)], axis=0
    ).astype(BF16)
    centers = jnp.broadcast_to(centers, (LANES, NBIN))
    step = lax.broadcasted_iota(jnp.int32, (LANES, NBIN), 0).astype(F32) + float(LANES)

    def hats(level):
        return jnp.maximum(0.0, 1.0 - jnp.abs(level - centers) / HW)

    for group in range(GROUPS):
        if group < BINADES:
            weights = hats(step * (2.0 ** -(group + 8)) * (NBIN - 1))
        elif group == BINADES:
            weights = jnp.maximum(0.0, 1.0 - centers / HW)
        elif group == BINADES + 1:
            weights = jnp.where(centers == 0.0, -1.0, jnp.where(centers <= 2.0, 1.0, 0.0))
        elif group == BINADES + 2:
            weights = jnp.where(centers == 3.0, 1.0, 0.0)
        elif group == BINADES + 3:
            weights = jnp.where(centers == 4.0, 1.0, 0.0)
        else:
            weights = hats(jnp.full((LANES, NBIN), float(NBIN - 1), F32))
        tab[:, group * LANES : (group + 1) * LANES] = lax.dot_general(
            copies, weights.astype(BF16), (((1,), (1,)), ((), ())), preferred_element_type=F32
        )


def lookup(values, tab):
    masks = [values >= 2.0 ** -(k + 1) for k in range(BINADES)]
    scale = jnp.full(values.shape, 2.0 ** (BINADES + 7), F32)
    for k in range(BINADES - 2, -1, -1):
        scale = jnp.where(masks[k], 2.0 ** (k + 8), scale)
    index = (values * scale).astype(jnp.int32) & (LANES - 1)
    quarter = values * ((NBIN - 1) / 4.0)
    coarse = (quarter + 1.5 * 2.0**15) - 1.5 * 2.0**15
    fine = (quarter + 1.5 * 2.0**14) - 1.5 * 2.0**14
    finest = quarter.astype(BF16).astype(F32)
    top = values >= 1.0
    out = []
    for c in range(4):

        def entry(group):
            return tab[8 * c : 8 * c + 8, group * LANES : (group + 1) * LANES]

        total = entry(BINADES) + coarse * entry(BINADES + 1)
        total = total + fine * entry(BINADES + 2) + finest * entry(BINADES + 3)
        for k in range(BINADES - 1, -1, -1):
            total = jnp.where(masks[k], jnp.take_along_axis(entry(k), index, axis=1), total)
        out.append(jnp.where(top, entry(BINADES + 4), total))
    return out


def body(sizes, vol, center_ref, table_ref, out, tab, xsd, look, zhalo, face, faces, rows_out, rows_in, part, recv1, recv2, bit_a,
         zs, zr, fs, fr, rs, rr, es, er, us, ur, ds, dr, ys, yr, cs, cr, qs, qr):
    nx, ny, nz = sizes
    planes, height, across = vol.shape
    ix, iy, iz = lax.axis_index("gx"), lax.axis_index("gy"), lax.axis_index("gz")
    depth = planes * nz

    def at(x, y, z):
        return (x, y, z)

    relations = []
    for s in (-1, 1):
        relations.append((((ix + s >= 0) & (ix + s < nx)), (ix + s, iy, iz)))
        relations.append((((iz + s >= 0) & (iz + s < nz)), (ix, iy, iz + s)))
    for s in (-1, 1):
        for t in (-1, 0, 1):
            relations.append(
                ((iy + s >= 0) & (iy + s < ny) & (ix + t >= 0) & (ix + t < nx), (ix + t, iy + s, iz))
            )
    bit0, bit1 = iz % 2, iz // 2
    near = iz + 1 - 2 * bit0
    far = iz + 2 - 4 * bit1
    faces[...] = jnp.zeros_like(faces)
    rows_in[...] = jnp.zeros_like(rows_in)
    barrier = pltpu.get_barrier_semaphore()
    count = 2
    for there, where in relations:
        count = count + there.astype(jnp.int32)

        @pl.when(there)
        def _(where=where):
            pl.semaphore_signal(barrier, inc=1, device_id=where, device_id_type=MESH)

    for where in ((ix, iy, near), (ix, iy, far)):
        pl.semaphore_signal(barrier, inc=1, device_id=where, device_id_type=MESH)
    pl.semaphore_wait(barrier, count)

    def remote(src, dst, ssem, rsem, where):
        return pltpu.make_async_remote_copy(
            src_ref=src, dst_ref=dst, send_sem=ssem, recv_sem=rsem, device_id=where, device_id_type=MESH
        )

    front, back = iz > 0, iz < nz - 1
    to_back = remote(vol.at[planes - 1], zhalo.at[0], zs.at[0], zr.at[0], (ix, iy, iz + 1))
    to_front = remote(vol.at[0], zhalo.at[1], zs.at[1], zr.at[1], (ix, iy, iz - 1))

    @pl.when(back)
    def _():
        to_back.start()

    @pl.when(front)
    def _():
        to_front.start()

    build_tables(center_ref, table_ref, tab)

    source = lax.broadcasted_iota(jnp.int32, (across, across), 0)
    target = lax.broadcasted_iota(jnp.int32, (across, across), 1)
    gap = source - target
    blur = jnp.where(gap == 0, 2.0, jnp.where(jnp.abs(gap) == 1, 1.0, 0.0))
    slope = jnp.where(gap == 1, 1.0, jnp.where(gap == -1, -1.0, 0.0))
    stencil = jnp.concatenate([blur, slope], axis=1).astype(BF16)

    def edge_columns(cells, plane):
        right = jnp.where((source == across - 1) & (target == 2 * plane + 1), 1.0, 0.0)
        left = jnp.where((source == 0) & (target == 2 * plane), 1.0, 0.0)
        return jnp.dot(cells, (right + left).astype(BF16), preferred_element_type=F32)

    def own_plane(z, acc):
        cells = vol[z]
        xsd[z + 1, pl.ds(8, height), :] = jnp.dot(cells, stencil, preferred_element_type=F32)
        return acc + edge_columns(cells, z + 1)

    columns = lax.fori_loop(0, planes, own_plane, jnp.zeros((height, across), F32))

    @pl.when(back)
    def _():
        to_back.wait_send()
        to_front.wait_recv()

    @pl.when(front)
    def _():
        to_front.wait_send()
        to_back.wait_recv()

    @pl.when(jnp.logical_not(front))
    def _():
        zhalo[0] = jnp.zeros_like(zhalo[0])

    @pl.when(jnp.logical_not(back))
    def _():
        zhalo[1] = jnp.zeros_like(zhalo[1])

    for slot, plane in ((0, 0), (1, planes + 1)):
        cells = zhalo[slot]
        xsd[plane, pl.ds(8, height), :] = jnp.dot(cells, stencil, preferred_element_type=F32)
        columns = columns + edge_columns(cells, plane)
    face[...] = columns.astype(BF16)

    def edge_rows(row):
        own = vol[:, row, :].astype(F32)
        pad = jnp.zeros((rows_out.shape[1] - planes - 2, across), F32)
        ends = [zhalo[slot, row : row + 1, :].astype(F32) for slot in (0, 1)]
        return jnp.concatenate([ends[0], own, ends[1], pad], axis=0).astype(BF16)

    rows_out[0] = edge_rows(0)
    rows_out[1] = edge_rows(height - 1)

    halo = []
    for s, slot in ((1, 0), (-1, 1)):
        sending = (ix + s >= 0) & (ix + s < nx)
        taking = (ix - s >= 0) & (ix - s < nx)
        halo.append((sending, taking, remote(face, faces.at[slot], fs.at[slot], fr.at[slot], (ix + s, iy, iz))))
    for s, side in ((1, 0), (-1, 1)):
        for t in (-1, 0, 1):
            slot = 1 - t
            sending = (iy + s >= 0) & (iy + s < ny) & (ix + t >= 0) & (ix + t < nx)
            taking = (iy - s >= 0) & (iy - s < ny) & (ix - t >= 0) & (ix - t < nx)
            halo.append(
                (sending, taking, remote(rows_out.at[1 - side], rows_in.at[side, slot], rs.at[side, slot], rr.at[side, slot], (ix + t, iy + s, iz)))
            )
    for sending, _, copy in halo:

        @pl.when(sending)
        def _(copy=copy):
            copy.start()

    tall = 16

    def look_block(n, carry):
        z = n // (height // tall)
        row = pl.multiple_of((n % (height // tall)) * tall, tall)
        cells = vol[z, pl.ds(row, tall), :].astype(F32)
        for half in range(tall // 8):
            four = lookup(cells[8 * half : 8 * half + 8], tab)
            for c in range(4):
                look[c, z, pl.ds(row + 8 * half, 8), :] = four[c]
        return carry

    lax.fori_loop(0, planes * (height // tall), look_block, 0)

    for sending, taking, copy in halo:

        @pl.when(taking)
        def _(copy=copy):
            copy.wait_recv()

        @pl.when(sending)
        def _(copy=copy):
            copy.wait_send()

    lane = lax.broadcasted_iota(jnp.int32, (height, across), 1)
    both = jnp.where(lane % 2 == 1, faces[0].astype(F32), faces[1].astype(F32))
    ends = jnp.where((lane == 0) | (lane == across - 1), 1.0, 0.0)
    sign = jnp.where(lane == 0, -1.0, jnp.where(lane == across - 1, 1.0, 0.0))

    def add_columns(z, carry):
        placed = pltpu.roll(both, across - 2 * z - 1, 1)
        xsd[z, pl.ds(8, height), :] += jnp.concatenate([placed * ends, placed * sign], axis=1)
        return carry

    lax.fori_loop(0, planes + 2, add_columns, 0)
    count_rows = rows_out.shape[1]
    for side in (0, 1):
        strip = jnp.dot(rows_in[side, 1], stencil, preferred_element_type=F32)
        left = pltpu.roll(rows_in[side, 0].astype(F32), 1, 1)
        right = pltpu.roll(rows_in[side, 2].astype(F32), across - 1, 1)
        short = lax.broadcasted_iota(jnp.int32, (count_rows, across), 1)
        left = jnp.where(short == 0, left, 0.0)
        right = jnp.where(short == across - 1, right, 0.0)
        strip = strip + jnp.concatenate([left + right, right - left], axis=1)
        row = 7 if side == 0 else 8 + height
        for z in range(planes + 2):
            xsd[z, row : row + 1, :] = strip[z : z + 1]

    shade_scale = (1.0 - ambient) / (32.0 * 3.0**0.5)

    sub = lax.broadcasted_iota(jnp.int32, (8, 2 * across), 0)

    def march(row):
        def gradients(z):
            above = xsd[z, pl.ds(row, 8), :]
            mid = xsd[z, pl.ds(row + 8, 8), :]
            below = xsd[z, pl.ds(row + 16, 8), :]
            up = pltpu.roll(jnp.where(sub == 7, above, mid), 1, 0)
            down = pltpu.roll(jnp.where(sub == 0, below, mid), 7, 0)
            smoothed = up + 2.0 * mid + down
            return smoothed[:, across:], down[:, :across] - up[:, :across], smoothed[:, :across]

        through = jnp.ones((8, across), F32)
        sums = [jnp.zeros((8, across), F32) for _ in range(3)]
        before, here = gradients(0), gradients(1)
        for z in range(planes):
            after = gradients(z + 2)
            grad_x = before[0] + 2.0 * here[0] + after[0]
            grad_y = before[1] + 2.0 * here[1] + after[1]
            grad_z = after[2] - before[2]
            before, here = here, after
            square = (grad_x * grad_x + grad_y * grad_y + grad_z * grad_z) * (1.0 / 1024.0) + grad_floor
            shade = ambient + shade_scale * jnp.abs(grad_x + grad_y + grad_z) * lax.rsqrt(square)
            clear = jnp.exp(look[3, z, pl.ds(row, 8), :] * (-depth_scale / depth))
            weight = through * (1.0 - clear) * shade
            for c in range(3):
                sums[c] = sums[c] + weight * look[c, z, pl.ds(row, 8), :]
            through = through * clear
        for c in range(3):
            part[c, pl.ds(row, 8), :] = sums[c]
        part[3, pl.ds(row, 8), :] = through

    half = height // 2
    band = height // 4
    keep = bit0 * half
    give = (1 - bit0) * half

    def march_half(start):
        def step(n, carry):
            march(pl.multiple_of(start + 8 * n, 8))
            return carry

        lax.fori_loop(0, half // 8, step, 0)

    march_half(give)
    first = remote(part.at[:, pl.ds(pl.multiple_of(give, half), half), :], recv1, es.at[0], er.at[0], (ix, iy, near))
    first.start()
    march_half(keep)
    first.wait_recv()

    def fold(mine, theirs, i_am_front):
        ahead = jnp.where(i_am_front, mine[3], theirs[3])
        mixed = []
        for c in range(3):
            a = jnp.where(i_am_front, mine[c], theirs[c])
            b = jnp.where(i_am_front, theirs[c], mine[c])
            mixed.append(a + ahead * b)
        mixed.append(mine[3] * theirs[3])
        return mixed

    pair = fold([part[c, pl.ds(pl.multiple_of(keep, half), half), :] for c in range(4)], [recv1[c] for c in range(4)], bit0 == 0)
    for c in range(4):
        bit_a[c] = pair[c]
    keep2 = pl.multiple_of(bit1 * band, band)
    give2 = pl.multiple_of((1 - bit1) * band, band)
    second = remote(bit_a.at[:, pl.ds(give2, band), :], recv2, es.at[1], er.at[1], (ix, iy, far))
    second.start()
    second.wait_recv()
    quad = fold([bit_a[c, pl.ds(keep2, band), :] for c in range(4)], [recv2[c] for c in range(4)], bit1 == 0)
    quad[3] = 1.0 - quad[3]

    def region(j, z):
        b = (z % 2) * 2 + z // 2
        return out.at[:, pl.ds(pl.multiple_of(b * band, band), band), pl.ds(pl.multiple_of(j * across, across), across)]

    mine_ref = region(ix, iz)
    for c in range(4):
        mine_ref[c] = quad[c]

    def up(j, t):
        return remote(region(j, iz), region(j, iz), us.at[t], ur.at[t], (ix + 1, iy, iz))

    def down(j, t):
        return remote(region(j, iz), region(j, iz), ds.at[t], dr.at[t], (ix - 1, iy, iz))

    def over(j, slot):
        return remote(region(j, iz), region(j, iz), ys.at[slot], yr.at[slot], (ix, iy, far))

    def side(j, slot):
        return remote(region(j, iz), region(j, iz), cs.at[slot], cr.at[slot], (ix, iy, near))

    def side_far(j, slot):
        return remote(region(j, far), region(j, far), qs.at[slot], qr.at[slot], (ix, iy, near))

    def take_over(j, slot):
        return remote(region(j, far), region(j, far), ys.at[slot], yr.at[slot], (ix, iy, far))

    far_near = near + 2 - 4 * bit1

    def spread(j, t, slot, upward, downward):
        if upward and t < nx - 1:

            @pl.when(ix + 1 < nx)
            def _():
                up(j, t).start()

        if downward and t < nx - 1:

            @pl.when(ix >= 1)
            def _():
                down(j, t).start()

        over(j, slot).start()
        side(j, slot).start()

    def relay(j, slot):
        take_over(j, slot).wait_recv()
        side_far(j, slot).start()

    spread(ix, 0, 0, True, True)
    for t in range(1, nx):

        @pl.when(ix >= t)
        def _(t=t):
            up(ix - t, t - 1).wait_recv()
            spread(ix - t, t, 2 * t - 1, True, False)

        @pl.when(ix + t < nx)
        def _(t=t):
            down(ix + t, t - 1).wait_recv()
            spread(ix + t, t, 2 * t, False, True)

        if t == 1:
            relay(ix, 0)
        else:

            @pl.when(ix >= t - 1)
            def _(t=t):
                relay(ix - t + 1, 2 * t - 3)

            @pl.when(ix + t - 1 < nx)
            def _(t=t):
                relay(ix + t - 1, 2 * t - 2)

    if nx == 1:
        relay(ix, 0)
    else:

        @pl.when(ix >= nx - 1)
        def _():
            relay(ix - nx + 1, 2 * nx - 3)

        @pl.when(ix + nx - 1 < nx)
        def _():
            relay(ix + nx - 1, 2 * nx - 2)

    def finish(j, slot):
        over(j, slot).wait_send()
        side(j, slot).wait_send()
        side_far(j, slot).wait_send()
        remote(region(j, near), region(j, near), cs.at[slot], cr.at[slot], (ix, iy, near)).wait_recv()
        remote(region(j, far_near), region(j, far_near), qs.at[slot], qr.at[slot], (ix, iy, near)).wait_recv()

    finish(ix, 0)
    for t in range(1, nx):

        @pl.when(ix >= t)
        def _(t=t):
            finish(ix - t, 2 * t - 1)

        @pl.when(ix + t < nx)
        def _(t=t):
            finish(ix + t, 2 * t)

    for t in range(nx - 1):

        @pl.when((ix >= t) & (ix + 1 < nx))
        def _(t=t):
            up(ix - t, t).wait_send()

        @pl.when((ix + t < nx) & (ix >= 1))
        def _(t=t):
            down(ix + t, t).wait_send()

    first.wait_send()
    second.wait_send()


def shards(volume, hat_center, tf_table):
    planes, height, across = volume.shape
    sizes = tuple(lax.axis_size(a) for a in ("gx", "gy", "gz"))
    nx = sizes[0]
    assert sizes[2] == 4 and across == LANES
    extended_rows = -(-(planes + 2) // 16) * 16
    dma = pltpu.SemaphoreType.DMA
    vmem = pl.BlockSpec(memory_space=pltpu.VMEM)
    return pl.pallas_call(
        functools.partial(body, sizes),
        out_shape=jax.ShapeDtypeStruct((4, height, across * nx), F32),
        in_specs=[vmem] * 3,
        out_specs=vmem,
        scratch_shapes=[
            pltpu.VMEM((32, GROUPS * LANES), F32),
            pltpu.VMEM((planes + 2, height + 16, 2 * across), F32),
            pltpu.VMEM((4, planes, height, across), F32),
            pltpu.VMEM((2, height, across), BF16),
            pltpu.VMEM((height, across), BF16),
            pltpu.VMEM((2, height, across), BF16),
            pltpu.VMEM((2, extended_rows, across), BF16),
            pltpu.VMEM((2, 3, extended_rows, across), BF16),
            pltpu.VMEM((4, height, across), F32),
            pltpu.VMEM((4, height // 2, across), F32),
            pltpu.VMEM((4, height // 4, across), F32),
            pltpu.VMEM((4, height // 2, across), F32),
            dma((2,)), dma((2,)),
            dma((2,)), dma((2,)),
            dma((2, 3)), dma((2, 3)),
            dma((2,)), dma((2,)),
            dma((nx,)), dma((nx,)),
            dma((nx,)), dma((nx,)),
            dma((2 * nx,)), dma((2 * nx,)),
            dma((2 * nx,)), dma((2 * nx,)),
            dma((2 * nx,)), dma((2 * nx,)),
        ],
        compiler_params=pltpu.CompilerParams(collective_id=0, has_side_effects=True, vmem_limit_bytes=48 << 20),
    )(volume, hat_center.reshape(1, -1), tf_table)


def solution(mesh):
    in_specs = (P("gz", "gy", "gx"), P(), P())
    out_specs = P(None, "gy", None)
    return jax.shard_map(shards, mesh=mesh, in_specs=in_specs, out_specs=out_specs, check_vma=False)
```

```python
import functools

import jax
import jax.numpy as jnp
from jax import lax
from jax.experimental import pallas as pl
from jax.experimental.pallas import tpu as pltpu
from jax.sharding import PartitionSpec as P

NBIN = 256
HW = 4

ambient = 0.3
grad_floor = 0.01
depth_scale = 1.5

LANES = 128
GROUPS = 7
MESH = pl.DeviceIdType.MESH
F32 = jnp.float32
BF16 = jnp.bfloat16


def build_tables(center_ref, table_ref, tab):
    centers = center_ref[...].astype(F32)
    wide = table_ref[...].astype(F32)
    copies = jnp.concatenate(
        [jnp.broadcast_to(wide[c : c + 1], (8, NBIN)) for c in range(4)], axis=0
    ).astype(BF16)
    centers = jnp.broadcast_to(centers, (LANES, NBIN))
    row = lax.broadcasted_iota(jnp.int32, (LANES, NBIN), 0).astype(F32)
    away = centers - row

    def hats(level):
        return jnp.maximum(0.0, 1.0 - jnp.abs(level - centers) / HW)

    groups = [
        hats((row + LANES) * (1.0 / (2 * LANES)) * (NBIN - 1)),
        jnp.where(away == -3.0, 0.0, jnp.maximum(0.0, 1.0 - jnp.abs(away) / HW)),
        jnp.where((away == 1.0) | (away == 2.0), 1.0, jnp.where((away == 0.0) | (away == -1.0), -1.0, 0.0)),
        jnp.where(away == 3.0, 1.0, jnp.where(away == -2.0, -1.0, 0.0)),
        jnp.where(away == 4.0, 1.0, 0.0),
        jnp.where(away == -3.0, 1.0, 0.0),
        hats(jnp.full((LANES, NBIN), float(NBIN - 1), F32)),
    ]
    for group, weights in enumerate(groups):
        tab[:, group * LANES : (group + 1) * LANES] = lax.dot_general(
            copies, weights.astype(BF16), (((1,), (1,)), ((), ())), preferred_element_type=F32
        )


def lookup(values, tab):
    level = values * float(NBIN - 1)
    bin_index = level.astype(jnp.int32)
    part_bin = level - bin_index.astype(F32)
    quarter = part_bin * 0.25
    coarse = (quarter + 1.5 * 2.0**15) - 1.5 * 2.0**15
    fine = (quarter + 1.5 * 2.0**14) - 1.5 * 2.0**14
    rising = quarter.astype(BF16).astype(F32)
    falling = ((1.0 - part_bin) * 0.25).astype(BF16).astype(F32)
    low_index = bin_index & (LANES - 1)
    high_index = (values * float(2 * LANES)).astype(jnp.int32) & (LANES - 1)
    upper, top = values >= 0.5, values >= 1.0

    def entry(c, group):
        return tab[8 * c : 8 * c + 8, group * LANES : (group + 1) * LANES]

    out = []
    for c in range(4):
        flat, per_coarse, per_fine, per_rising, per_falling = (
            jnp.take_along_axis(entry(c, 1 + k), low_index, axis=1) for k in range(5)
        )
        total = (flat + coarse * per_coarse) + (fine * per_fine + rising * per_rising + falling * per_falling)
        out.append(total)
    for c in range(4):
        high = jnp.take_along_axis(entry(c, 0), high_index, axis=1)
        out[c] = jnp.where(top, entry(c, 6), jnp.where(upper, high, out[c]))
    return out


def body(sizes, vol, center_ref, table_ref, out, tab, xsd, look, zhalo, face, faces, rows_out, rows_in, part, recv1, recv2, bit_a,
         zs, zr, fs, fr, rs, rr, es, er, us, ur, ds, dr, ys, yr, cs, cr, qs, qr):
    nx, ny, nz = sizes
    planes, height, across = vol.shape
    ix, iy, iz = lax.axis_index("gx"), lax.axis_index("gy"), lax.axis_index("gz")
    depth = planes * nz

    def at(x, y, z):
        return (x, y, z)

    relations = []
    for s in (-1, 1):
        relations.append((((ix + s >= 0) & (ix + s < nx)), (ix + s, iy, iz)))
        relations.append((((iz + s >= 0) & (iz + s < nz)), (ix, iy, iz + s)))
    for s in (-1, 1):
        for t in (-1, 0, 1):
            relations.append(
                ((iy + s >= 0) & (iy + s < ny) & (ix + t >= 0) & (ix + t < nx), (ix + t, iy + s, iz))
            )
    bit0, bit1 = iz % 2, iz // 2
    near = iz + 1 - 2 * bit0
    far = iz + 2 - 4 * bit1
    faces[...] = jnp.zeros_like(faces)
    rows_in[...] = jnp.zeros_like(rows_in)
    barrier = pltpu.get_barrier_semaphore()
    count = 2
    for there, where in relations:
        count = count + there.astype(jnp.int32)

        @pl.when(there)
        def _(where=where):
            pl.semaphore_signal(barrier, inc=1, device_id=where, device_id_type=MESH)

    for where in ((ix, iy, near), (ix, iy, far)):
        pl.semaphore_signal(barrier, inc=1, device_id=where, device_id_type=MESH)
    pl.semaphore_wait(barrier, count)

    def remote(src, dst, ssem, rsem, where):
        return pltpu.make_async_remote_copy(
            src_ref=src, dst_ref=dst, send_sem=ssem, recv_sem=rsem, device_id=where, device_id_type=MESH
        )

    front, back = iz > 0, iz < nz - 1
    to_back = remote(vol.at[planes - 1], zhalo.at[0], zs.at[0], zr.at[0], (ix, iy, iz + 1))
    to_front = remote(vol.at[0], zhalo.at[1], zs.at[1], zr.at[1], (ix, iy, iz - 1))

    @pl.when(back)
    def _():
        to_back.start()

    @pl.when(front)
    def _():
        to_front.start()

    build_tables(center_ref, table_ref, tab)

    source = lax.broadcasted_iota(jnp.int32, (across, across), 0)
    target = lax.broadcasted_iota(jnp.int32, (across, across), 1)
    gap = source - target
    blur = jnp.where(gap == 0, 2.0, jnp.where(jnp.abs(gap) == 1, 1.0, 0.0))
    slope = jnp.where(gap == 1, 1.0, jnp.where(gap == -1, -1.0, 0.0))
    stencil = jnp.concatenate([blur, slope], axis=1).astype(BF16)

    def edge_columns(cells, plane):
        right = jnp.where((source == across - 1) & (target == 2 * plane + 1), 1.0, 0.0)
        left = jnp.where((source == 0) & (target == 2 * plane), 1.0, 0.0)
        return jnp.dot(cells, (right + left).astype(BF16), preferred_element_type=F32)

    def own_plane(z, acc):
        cells = vol[z]
        xsd[z + 1, pl.ds(8, height), :] = jnp.dot(cells, stencil, preferred_element_type=F32)
        return acc + edge_columns(cells, z + 1)

    columns = lax.fori_loop(0, planes, own_plane, jnp.zeros((height, across), F32))

    @pl.when(back)
    def _():
        to_back.wait_send()
        to_front.wait_recv()

    @pl.when(front)
    def _():
        to_front.wait_send()
        to_back.wait_recv()

    @pl.when(jnp.logical_not(front))
    def _():
        zhalo[0] = jnp.zeros_like(zhalo[0])

    @pl.when(jnp.logical_not(back))
    def _():
        zhalo[1] = jnp.zeros_like(zhalo[1])

    for slot, plane in ((0, 0), (1, planes + 1)):
        cells = zhalo[slot]
        xsd[plane, pl.ds(8, height), :] = jnp.dot(cells, stencil, preferred_element_type=F32)
        columns = columns + edge_columns(cells, plane)
    face[...] = columns.astype(BF16)

    def edge_rows(row):
        own = vol[:, row, :].astype(F32)
        pad = jnp.zeros((rows_out.shape[1] - planes - 2, across), F32)
        ends = [zhalo[slot, row : row + 1, :].astype(F32) for slot in (0, 1)]
        return jnp.concatenate([ends[0], own, ends[1], pad], axis=0).astype(BF16)

    rows_out[0] = edge_rows(0)
    rows_out[1] = edge_rows(height - 1)

    halo = []
    for s, slot in ((1, 0), (-1, 1)):
        sending = (ix + s >= 0) & (ix + s < nx)
        taking = (ix - s >= 0) & (ix - s < nx)
        halo.append((sending, taking, remote(face, faces.at[slot], fs.at[slot], fr.at[slot], (ix + s, iy, iz))))
    for s, side in ((1, 0), (-1, 1)):
        for t in (-1, 0, 1):
            slot = 1 - t
            sending = (iy + s >= 0) & (iy + s < ny) & (ix + t >= 0) & (ix + t < nx)
            taking = (iy - s >= 0) & (iy - s < ny) & (ix - t >= 0) & (ix - t < nx)
            halo.append(
                (sending, taking, remote(rows_out.at[1 - side], rows_in.at[side, slot], rs.at[side, slot], rr.at[side, slot], (ix + t, iy + s, iz)))
            )
    for sending, _, copy in halo:

        @pl.when(sending)
        def _(copy=copy):
            copy.start()

    tall = 64

    def look_block(n, carry):
        z = n // (height // tall)
        row = pl.multiple_of((n % (height // tall)) * tall, tall)
        cells = vol[z, pl.ds(row, tall), :].astype(F32)
        for half in range(tall // 8):
            four = lookup(cells[8 * half : 8 * half + 8], tab)
            for c in range(4):
                look[c, z, pl.ds(row + 8 * half, 8), :] = four[c]
        return carry

    lax.fori_loop(0, planes * (height // tall), look_block, 0)

    for sending, taking, copy in halo:

        @pl.when(taking)
        def _(copy=copy):
            copy.wait_recv()

        @pl.when(sending)
        def _(copy=copy):
            copy.wait_send()

    lane = lax.broadcasted_iota(jnp.int32, (height, across), 1)
    both = jnp.where(lane % 2 == 1, faces[0].astype(F32), faces[1].astype(F32))
    ends = jnp.where((lane == 0) | (lane == across - 1), 1.0, 0.0)
    sign = jnp.where(lane == 0, -1.0, jnp.where(lane == across - 1, 1.0, 0.0))

    def add_columns(z, carry):
        placed = pltpu.roll(both, across - 2 * z - 1, 1)
        xsd[z, pl.ds(8, height), :] += jnp.concatenate([placed * ends, placed * sign], axis=1)
        return carry

    lax.fori_loop(0, planes + 2, add_columns, 0)
    count_rows = rows_out.shape[1]
    for side in (0, 1):
        strip = jnp.dot(rows_in[side, 1], stencil, preferred_element_type=F32)
        left = pltpu.roll(rows_in[side, 0].astype(F32), 1, 1)
        right = pltpu.roll(rows_in[side, 2].astype(F32), across - 1, 1)
        short = lax.broadcasted_iota(jnp.int32, (count_rows, across), 1)
        left = jnp.where(short == 0, left, 0.0)
        right = jnp.where(short == across - 1, right, 0.0)
        strip = strip + jnp.concatenate([left + right, right - left], axis=1)
        row = 7 if side == 0 else 8 + height
        for z in range(planes + 2):
            xsd[z, row : row + 1, :] = strip[z : z + 1]

    shade_scale = (1.0 - ambient) / (32.0 * 3.0**0.5)

    sub = lax.broadcasted_iota(jnp.int32, (8, 2 * across), 0)

    def march(row):
        def gradients(z):
            above = xsd[z, pl.ds(row, 8), :]
            mid = xsd[z, pl.ds(row + 8, 8), :]
            below = xsd[z, pl.ds(row + 16, 8), :]
            up = pltpu.roll(jnp.where(sub == 7, above, mid), 1, 0)
            down = pltpu.roll(jnp.where(sub == 0, below, mid), 7, 0)
            smoothed = up + 2.0 * mid + down
            return smoothed[:, across:], down[:, :across] - up[:, :across], smoothed[:, :across]

        through = jnp.ones((8, across), F32)
        sums = [jnp.zeros((8, across), F32) for _ in range(3)]
        before, here = gradients(0), gradients(1)
        for z in range(planes):
            after = gradients(z + 2)
            grad_x = before[0] + 2.0 * here[0] + after[0]
            grad_y = before[1] + 2.0 * here[1] + after[1]
            grad_z = after[2] - before[2]
            before, here = here, after
            square = (grad_x * grad_x + grad_y * grad_y + grad_z * grad_z) * (1.0 / 1024.0) + grad_floor
            shade = ambient + shade_scale * jnp.abs(grad_x + grad_y + grad_z) * lax.rsqrt(square)
            clear = jnp.exp(look[3, z, pl.ds(row, 8), :] * (-depth_scale / depth))
            weight = through * (1.0 - clear) * shade
            for c in range(3):
                sums[c] = sums[c] + weight * look[c, z, pl.ds(row, 8), :]
            through = through * clear
        for c in range(3):
            part[c, pl.ds(row, 8), :] = sums[c]
        part[3, pl.ds(row, 8), :] = through

    half = height // 2
    band = height // 4
    keep = bit0 * half
    give = (1 - bit0) * half

    def march_half(start):
        def step(n, carry):
            march(pl.multiple_of(start + 8 * n, 8))
            return carry

        lax.fori_loop(0, half // 8, step, 0)

    march_half(give)
    first = remote(part.at[:, pl.ds(pl.multiple_of(give, half), half), :], recv1, es.at[0], er.at[0], (ix, iy, near))
    first.start()
    march_half(keep)
    first.wait_recv()

    def fold(mine, theirs, i_am_front):
        ahead = jnp.where(i_am_front, mine[3], theirs[3])
        mixed = []
        for c in range(3):
            a = jnp.where(i_am_front, mine[c], theirs[c])
            b = jnp.where(i_am_front, theirs[c], mine[c])
            mixed.append(a + ahead * b)
        mixed.append(mine[3] * theirs[3])
        return mixed

    pair = fold([part[c, pl.ds(pl.multiple_of(keep, half), half), :] for c in range(4)], [recv1[c] for c in range(4)], bit0 == 0)
    for c in range(4):
        bit_a[c] = pair[c]
    keep2 = pl.multiple_of(bit1 * band, band)
    give2 = pl.multiple_of((1 - bit1) * band, band)
    second = remote(bit_a.at[:, pl.ds(give2, band), :], recv2, es.at[1], er.at[1], (ix, iy, far))
    second.start()
    second.wait_recv()
    quad = fold([bit_a[c, pl.ds(keep2, band), :] for c in range(4)], [recv2[c] for c in range(4)], bit1 == 0)
    quad[3] = 1.0 - quad[3]

    def region(j, z):
        b = (z % 2) * 2 + z // 2
        return out.at[:, pl.ds(pl.multiple_of(b * band, band), band), pl.ds(pl.multiple_of(j * across, across), across)]

    mine_ref = region(ix, iz)
    for c in range(4):
        mine_ref[c] = quad[c]

    def up(j, t):
        return remote(region(j, iz), region(j, iz), us.at[t], ur.at[t], (ix + 1, iy, iz))

    def down(j, t):
        return remote(region(j, iz), region(j, iz), ds.at[t], dr.at[t], (ix - 1, iy, iz))

    def over(j, slot):
        return remote(region(j, iz), region(j, iz), ys.at[slot], yr.at[slot], (ix, iy, far))

    def side(j, slot):
        return remote(region(j, iz), region(j, iz), cs.at[slot], cr.at[slot], (ix, iy, near))

    def side_far(j, slot):
        return remote(region(j, far), region(j, far), qs.at[slot], qr.at[slot], (ix, iy, near))

    def take_over(j, slot):
        return remote(region(j, far), region(j, far), ys.at[slot], yr.at[slot], (ix, iy, far))

    far_near = near + 2 - 4 * bit1

    def spread(j, t, slot, upward, downward):
        if upward and t < nx - 1:

            @pl.when(ix + 1 < nx)
            def _():
                up(j, t).start()

        if downward and t < nx - 1:

            @pl.when(ix >= 1)
            def _():
                down(j, t).start()

        over(j, slot).start()
        side(j, slot).start()

    def relay(j, slot):
        take_over(j, slot).wait_recv()
        side_far(j, slot).start()

    spread(ix, 0, 0, True, True)
    for t in range(1, nx):

        @pl.when(ix >= t)
        def _(t=t):
            up(ix - t, t - 1).wait_recv()
            spread(ix - t, t, 2 * t - 1, True, False)

        @pl.when(ix + t < nx)
        def _(t=t):
            down(ix + t, t - 1).wait_recv()
            spread(ix + t, t, 2 * t, False, True)

        if t == 1:
            relay(ix, 0)
        else:

            @pl.when(ix >= t - 1)
            def _(t=t):
                relay(ix - t + 1, 2 * t - 3)

            @pl.when(ix + t - 1 < nx)
            def _(t=t):
                relay(ix + t - 1, 2 * t - 2)

    if nx == 1:
        relay(ix, 0)
    else:

        @pl.when(ix >= nx - 1)
        def _():
            relay(ix - nx + 1, 2 * nx - 3)

        @pl.when(ix + nx - 1 < nx)
        def _():
            relay(ix + nx - 1, 2 * nx - 2)

    def finish(j, slot):
        over(j, slot).wait_send()
        side(j, slot).wait_send()
        side_far(j, slot).wait_send()
        remote(region(j, near), region(j, near), cs.at[slot], cr.at[slot], (ix, iy, near)).wait_recv()
        remote(region(j, far_near), region(j, far_near), qs.at[slot], qr.at[slot], (ix, iy, near)).wait_recv()

    finish(ix, 0)
    for t in range(1, nx):

        @pl.when(ix >= t)
        def _(t=t):
            finish(ix - t, 2 * t - 1)

        @pl.when(ix + t < nx)
        def _(t=t):
            finish(ix + t, 2 * t)

    for t in range(nx - 1):

        @pl.when((ix >= t) & (ix + 1 < nx))
        def _(t=t):
            up(ix - t, t).wait_send()

        @pl.when((ix + t < nx) & (ix >= 1))
        def _(t=t):
            down(ix + t, t).wait_send()

    first.wait_send()
    second.wait_send()


def shards(volume, hat_center, tf_table):
    planes, height, across = volume.shape
    sizes = tuple(lax.axis_size(a) for a in ("gx", "gy", "gz"))
    nx = sizes[0]
    assert sizes[2] == 4 and across == LANES
    extended_rows = -(-(planes + 2) // 16) * 16
    dma = pltpu.SemaphoreType.DMA
    vmem = pl.BlockSpec(memory_space=pltpu.VMEM)
    return pl.pallas_call(
        functools.partial(body, sizes),
        out_shape=jax.ShapeDtypeStruct((4, height, across * nx), F32),
        in_specs=[vmem] * 3,
        out_specs=vmem,
        scratch_shapes=[
            pltpu.VMEM((32, GROUPS * LANES), F32),
            pltpu.VMEM((planes + 2, height + 16, 2 * across), F32),
            pltpu.VMEM((4, planes, height, across), F32),
            pltpu.VMEM((2, height, across), BF16),
            pltpu.VMEM((height, across), BF16),
            pltpu.VMEM((2, height, across), BF16),
            pltpu.VMEM((2, extended_rows, across), BF16),
            pltpu.VMEM((2, 3, extended_rows, across), BF16),
            pltpu.VMEM((4, height, across), F32),
            pltpu.VMEM((4, height // 2, across), F32),
            pltpu.VMEM((4, height // 4, across), F32),
            pltpu.VMEM((4, height // 2, across), F32),
            dma((2,)), dma((2,)),
            dma((2,)), dma((2,)),
            dma((2, 3)), dma((2, 3)),
            dma((2,)), dma((2,)),
            dma((nx,)), dma((nx,)),
            dma((nx,)), dma((nx,)),
            dma((2 * nx,)), dma((2 * nx,)),
            dma((2 * nx,)), dma((2 * nx,)),
            dma((2 * nx,)), dma((2 * nx,)),
        ],
        compiler_params=pltpu.CompilerParams(collective_id=0, has_side_effects=True, vmem_limit_bytes=48 << 20),
    )(volume, hat_center.reshape(1, -1), tf_table)


def solution(mesh):
    in_specs = (P("gz", "gy", "gx"), P(), P())
    out_specs = P(None, "gy", None)
    return jax.shard_map(shards, mesh=mesh, in_specs=in_specs, out_specs=out_specs, check_vma=False)
```

```python
import functools

import jax
import jax.numpy as jnp
from jax import lax
from jax.experimental import pallas as pl
from jax.experimental.pallas import tpu as pltpu
from jax.sharding import PartitionSpec as P

NBIN = 256
HW = 4

ambient = 0.3
grad_floor = 0.01
depth_scale = 1.5

LANES = 128
GROUPS = 7
MESH = pl.DeviceIdType.MESH
F32 = jnp.float32
BF16 = jnp.bfloat16


def build_tables(center_ref, table_ref, tab):
    centers = center_ref[...].astype(F32)
    wide = table_ref[...].astype(F32)
    copies = jnp.concatenate(
        [jnp.broadcast_to(wide[c : c + 1], (8, NBIN)) for c in range(4)], axis=0
    ).astype(BF16)
    centers = jnp.broadcast_to(centers, (LANES, NBIN))
    row = lax.broadcasted_iota(jnp.int32, (LANES, NBIN), 0).astype(F32)
    away = centers - row

    def hats(level):
        return jnp.maximum(0.0, 1.0 - jnp.abs(level - centers) / HW)

    groups = [
        hats((row + LANES) * (1.0 / (2 * LANES)) * (NBIN - 1)),
        jnp.where(away == -3.0, 0.0, jnp.maximum(0.0, 1.0 - jnp.abs(away) / HW)),
        jnp.where((away == 1.0) | (away == 2.0), 1.0, jnp.where((away == 0.0) | (away == -1.0), -1.0, 0.0)),
        jnp.where(away == 3.0, 1.0, jnp.where(away == -2.0, -1.0, 0.0)),
        jnp.where(away == 4.0, 1.0, 0.0),
        jnp.where(away == -3.0, 1.0, 0.0),
        hats(jnp.full((LANES, NBIN), float(NBIN - 1), F32)),
    ]
    for group, weights in enumerate(groups):
        tab[:, group * LANES : (group + 1) * LANES] = lax.dot_general(
            copies, weights.astype(BF16), (((1,), (1,)), ((), ())), preferred_element_type=F32
        )


def lookup(values, tab):
    level = values * float(NBIN - 1)
    bin_index = level.astype(jnp.int32)
    part_bin = level - bin_index.astype(F32)
    quarter = part_bin * 0.25
    coarse = (quarter + 1.5 * 2.0**15) - 1.5 * 2.0**15
    fine = (quarter + 1.5 * 2.0**14) - 1.5 * 2.0**14
    rising = quarter.astype(BF16).astype(F32)
    falling = ((1.0 - part_bin) * 0.25).astype(BF16).astype(F32)
    low_index = bin_index & (LANES - 1)
    high_index = (values * float(2 * LANES)).astype(jnp.int32) & (LANES - 1)
    upper, top = values >= 0.5, values >= 1.0

    def entry(c, group):
        return tab[8 * c : 8 * c + 8, group * LANES : (group + 1) * LANES]

    out = []
    for c in range(4):
        flat, per_coarse, per_fine, per_rising, per_falling = (
            jnp.take_along_axis(entry(c, 1 + k), low_index, axis=1) for k in range(5)
        )
        total = (flat + coarse * per_coarse) + (fine * per_fine + rising * per_rising + falling * per_falling)
        out.append(total)
    for c in range(4):
        high = jnp.take_along_axis(entry(c, 0), high_index, axis=1)
        out[c] = jnp.where(top, entry(c, 6), jnp.where(upper, high, out[c]))
    return out


def body(sizes, vol, center_ref, table_ref, out, tab, xsd, look_a, look_b, look_c, zhalo, face, faces, rows_out, rows_in, part, recv1, recv2, pair,
         zs, zr, fs, fr, rs, rr, es, er, us, ur, ds, dr, ys, yr, cs, cr, qs, qr):
    nx, ny, nz = sizes
    planes, height, across = vol.shape
    ix, iy, iz = lax.axis_index("gx"), lax.axis_index("gy"), lax.axis_index("gz")
    depth = planes * nz

    def at(x, y, z):
        return (x, y, z)

    relations = []
    for s in (-1, 1):
        relations.append((((ix + s >= 0) & (ix + s < nx)), (ix + s, iy, iz)))
        relations.append((((iz + s >= 0) & (iz + s < nz)), (ix, iy, iz + s)))
    for s in (-1, 1):
        for t in (-1, 0, 1):
            relations.append(
                ((iy + s >= 0) & (iy + s < ny) & (ix + t >= 0) & (ix + t < nx), (ix + t, iy + s, iz))
            )
    bit0, bit1 = iz % 2, iz // 2
    near = iz + 1 - 2 * bit0
    far = iz + 2 - 4 * bit1
    faces[...] = jnp.zeros_like(faces)
    rows_in[...] = jnp.zeros_like(rows_in)
    barrier = pltpu.get_barrier_semaphore()
    count = 2
    for there, where in relations:
        count = count + there.astype(jnp.int32)

        @pl.when(there)
        def _(where=where):
            pl.semaphore_signal(barrier, inc=1, device_id=where, device_id_type=MESH)

    for where in ((ix, iy, near), (ix, iy, far)):
        pl.semaphore_signal(barrier, inc=1, device_id=where, device_id_type=MESH)
    pl.semaphore_wait(barrier, count)

    def remote(src, dst, ssem, rsem, where):
        return pltpu.make_async_remote_copy(
            src_ref=src, dst_ref=dst, send_sem=ssem, recv_sem=rsem, device_id=where, device_id_type=MESH
        )

    front, back = iz > 0, iz < nz - 1
    to_back = remote(vol.at[planes - 1], zhalo.at[0], zs.at[0], zr.at[0], (ix, iy, iz + 1))
    to_front = remote(vol.at[0], zhalo.at[1], zs.at[1], zr.at[1], (ix, iy, iz - 1))

    @pl.when(back)
    def _():
        to_back.start()

    @pl.when(front)
    def _():
        to_front.start()

    build_tables(center_ref, table_ref, tab)

    source = lax.broadcasted_iota(jnp.int32, (across, across), 0)
    target = lax.broadcasted_iota(jnp.int32, (across, across), 1)
    gap = source - target
    blur = jnp.where(gap == 0, 2.0, jnp.where(jnp.abs(gap) == 1, 1.0, 0.0))
    slope = jnp.where(gap == 1, 1.0, jnp.where(gap == -1, -1.0, 0.0))
    stencil = jnp.concatenate([blur, slope], axis=1).astype(BF16)

    def edge_columns(cells, plane):
        right = jnp.where((source == across - 1) & (target == 2 * plane + 1), 1.0, 0.0)
        left = jnp.where((source == 0) & (target == 2 * plane), 1.0, 0.0)
        return jnp.dot(cells, (right + left).astype(BF16), preferred_element_type=F32)

    def own_plane(z, acc):
        cells = vol[z]
        xsd[z + 1, pl.ds(8, height), :] = jnp.dot(cells, stencil, preferred_element_type=F32)
        return acc + edge_columns(cells, z + 1)

    columns = lax.fori_loop(0, planes, own_plane, jnp.zeros((height, across), F32))

    @pl.when(back)
    def _():
        to_back.wait_send()
        to_front.wait_recv()

    @pl.when(front)
    def _():
        to_front.wait_send()
        to_back.wait_recv()

    @pl.when(jnp.logical_not(front))
    def _():
        zhalo[0] = jnp.zeros_like(zhalo[0])

    @pl.when(jnp.logical_not(back))
    def _():
        zhalo[1] = jnp.zeros_like(zhalo[1])

    for slot, plane in ((0, 0), (1, planes + 1)):
        cells = zhalo[slot]
        xsd[plane, pl.ds(8, height), :] = jnp.dot(cells, stencil, preferred_element_type=F32)
        columns = columns + edge_columns(cells, plane)
    face[...] = columns.astype(BF16)

    def edge_rows(row):
        own = vol[:, row, :].astype(F32)
        pad = jnp.zeros((rows_out.shape[1] - planes - 2, across), F32)
        ends = [zhalo[slot, row : row + 1, :].astype(F32) for slot in (0, 1)]
        return jnp.concatenate([ends[0], own, ends[1], pad], axis=0).astype(BF16)

    rows_out[0] = edge_rows(0)
    rows_out[1] = edge_rows(height - 1)

    halo = []
    for s, slot in ((1, 0), (-1, 1)):
        sending = (ix + s >= 0) & (ix + s < nx)
        taking = (ix - s >= 0) & (ix - s < nx)
        halo.append((sending, taking, remote(face, faces.at[slot], fs.at[slot], fr.at[slot], (ix + s, iy, iz))))
    for s, side in ((1, 0), (-1, 1)):
        for t in (-1, 0, 1):
            slot = 1 - t
            sending = (iy + s >= 0) & (iy + s < ny) & (ix + t >= 0) & (ix + t < nx)
            taking = (iy - s >= 0) & (iy - s < ny) & (ix - t >= 0) & (ix - t < nx)
            halo.append(
                (sending, taking, remote(rows_out.at[1 - side], rows_in.at[side, slot], rs.at[side, slot], rr.at[side, slot], (ix + t, iy + s, iz)))
            )
    for sending, _, copy in halo:

        @pl.when(sending)
        def _(copy=copy):
            copy.start()

    half, band = height // 2, height // 4
    keep, give = bit0 * half, (1 - bit0) * half
    keep2, give2 = bit1 * band, (1 - bit1) * band

    def look_rows(table, z, start, count):
        cells = vol[z, pl.ds(pl.multiple_of(start, 16), count), :].astype(F32)
        for k in range(count // 8):
            four = lookup(cells[8 * k : 8 * k + 8], tab)
            for c in range(4):
                table[c, z, 8 * k : 8 * k + 8, :] = four[c]

    def look_give(z, carry):
        look_rows(look_a, z, give, half)
        return carry

    lax.fori_loop(0, planes, look_give, 0)

    for sending, taking, copy in halo:

        @pl.when(taking)
        def _(copy=copy):
            copy.wait_recv()

        @pl.when(sending)
        def _(copy=copy):
            copy.wait_send()

    lane = lax.broadcasted_iota(jnp.int32, (height, across), 1)
    both = jnp.where(lane % 2 == 1, faces[0].astype(F32), faces[1].astype(F32))
    ends = jnp.where((lane == 0) | (lane == across - 1), 1.0, 0.0)
    sign = jnp.where(lane == 0, -1.0, jnp.where(lane == across - 1, 1.0, 0.0))

    def add_columns(z, carry):
        placed = pltpu.roll(both, across - 2 * z - 1, 1)
        xsd[z, pl.ds(8, height), :] += jnp.concatenate([placed * ends, placed * sign], axis=1)
        return carry

    lax.fori_loop(0, planes + 2, add_columns, 0)
    count_rows = rows_out.shape[1]
    for side in (0, 1):
        strip = jnp.dot(rows_in[side, 1], stencil, preferred_element_type=F32)
        left = pltpu.roll(rows_in[side, 0].astype(F32), 1, 1)
        right = pltpu.roll(rows_in[side, 2].astype(F32), across - 1, 1)
        short = lax.broadcasted_iota(jnp.int32, (count_rows, across), 1)
        left = jnp.where(short == 0, left, 0.0)
        right = jnp.where(short == across - 1, right, 0.0)
        strip = strip + jnp.concatenate([left + right, right - left], axis=1)
        row = 7 if side == 0 else 8 + height
        for z in range(planes + 2):
            xsd[z, row : row + 1, :] = strip[z : z + 1]

    shade_scale = (1.0 - ambient) / (32.0 * 3.0**0.5)

    sub = lax.broadcasted_iota(jnp.int32, (8, 2 * across), 0)

    def march(row, table, own):
        def gradients(z):
            above = xsd[z, pl.ds(row, 8), :]
            mid = xsd[z, pl.ds(row + 8, 8), :]
            below = xsd[z, pl.ds(row + 16, 8), :]
            up = pltpu.roll(jnp.where(sub == 7, above, mid), 1, 0)
            down = pltpu.roll(jnp.where(sub == 0, below, mid), 7, 0)
            smoothed = up + 2.0 * mid + down
            return smoothed[:, across:], down[:, :across] - up[:, :across], smoothed[:, :across]

        through = jnp.ones((8, across), F32)
        sums = [jnp.zeros((8, across), F32) for _ in range(3)]
        before, here = gradients(0), gradients(1)
        for z in range(planes):
            after = gradients(z + 2)
            grad_x = before[0] + 2.0 * here[0] + after[0]
            grad_y = before[1] + 2.0 * here[1] + after[1]
            grad_z = after[2] - before[2]
            before, here = here, after
            square = (grad_x * grad_x + grad_y * grad_y + grad_z * grad_z) * (1.0 / 1024.0) + grad_floor
            shade = ambient + shade_scale * jnp.abs(grad_x + grad_y + grad_z) * lax.rsqrt(square)
            clear = jnp.exp(table[3, z, pl.ds(own, 8), :] * (-depth_scale / depth))
            weight = through * (1.0 - clear) * shade
            for c in range(3):
                sums[c] = sums[c] + weight * table[c, z, pl.ds(own, 8), :]
            through = through * clear
        for c in range(3):
            part[c, pl.ds(row, 8), :] = sums[c]
        part[3, pl.ds(row, 8), :] = through

    def march_rows(start, table, count, along=None):
        def step(n, carry):
            march(pl.multiple_of(start + 8 * n, 8), table, pl.multiple_of(8 * n, 8))
            if along is not None:
                along(n)
            return carry

        lax.fori_loop(0, count // 8, step, 0)

    share = planes // (half // 8)

    def look_give2(n):
        for k in range(share):
            look_rows(look_b, share * n + k, keep + give2, band)

    march_rows(give, look_a, half, look_give2)
    first = remote(part.at[:, pl.ds(pl.multiple_of(give, half), half), :], recv1, es.at[0], er.at[0], (ix, iy, near))
    first.start()
    march_rows(keep + give2, look_b, band)
    first.wait_recv()

    def fold(mine, theirs, i_am_front):
        ahead = jnp.where(i_am_front, mine[3], theirs[3])
        mixed = []
        for c in range(3):
            a = jnp.where(i_am_front, mine[c], theirs[c])
            b = jnp.where(i_am_front, theirs[c], mine[c])
            mixed.append(a + ahead * b)
        mixed.append(mine[3] * theirs[3])
        return mixed

    def pair_of(start):
        own = pl.ds(pl.multiple_of(keep + start, band), band)
        other = pl.ds(pl.multiple_of(start, band), band)
        return fold([part[c, own, :] for c in range(4)], [recv1[c, other, :] for c in range(4)], bit0 == 0)

    for c, value in enumerate(pair_of(give2)):
        pair[c] = value
    second = remote(pair, recv2, es.at[1], er.at[1], (ix, iy, far))
    second.start()

    def look_keep2(n, carry):
        for k in range(2):
            look_rows(look_c, 2 * n + k, keep + keep2, band)
        return carry

    lax.fori_loop(0, planes // 2, look_keep2, 0)
    march_rows(keep + keep2, look_c, band)
    mine = pair_of(keep2)
    second.wait_recv()
    quad = fold(mine, [recv2[c] for c in range(4)], bit1 == 0)
    quad[3] = 1.0 - quad[3]

    def region(j, z):
        b = (z % 2) * 2 + z // 2
        return out.at[:, pl.ds(pl.multiple_of(b * band, band), band), pl.ds(pl.multiple_of(j * across, across), across)]

    mine_ref = region(ix, iz)
    for c in range(4):
        mine_ref[c] = quad[c]

    def up(j, t):
        return remote(region(j, iz), region(j, iz), us.at[t], ur.at[t], (ix + 1, iy, iz))

    def down(j, t):
        return remote(region(j, iz), region(j, iz), ds.at[t], dr.at[t], (ix - 1, iy, iz))

    def over(j, slot):
        return remote(region(j, iz), region(j, iz), ys.at[slot], yr.at[slot], (ix, iy, far))

    def side(j, slot):
        return remote(region(j, iz), region(j, iz), cs.at[slot], cr.at[slot], (ix, iy, near))

    def side_far(j, slot):
        return remote(region(j, far), region(j, far), qs.at[slot], qr.at[slot], (ix, iy, near))

    def take_over(j, slot):
        return remote(region(j, far), region(j, far), ys.at[slot], yr.at[slot], (ix, iy, far))

    far_near = near + 2 - 4 * bit1

    def spread(j, t, slot, upward, downward):
        if upward and t < nx - 1:

            @pl.when(ix + 1 < nx)
            def _():
                up(j, t).start()

        if downward and t < nx - 1:

            @pl.when(ix >= 1)
            def _():
                down(j, t).start()

        over(j, slot).start()
        side(j, slot).start()

    def relay(j, slot):
        take_over(j, slot).wait_recv()
        side_far(j, slot).start()

    spread(ix, 0, 0, True, True)
    for t in range(1, nx):

        @pl.when(ix >= t)
        def _(t=t):
            up(ix - t, t - 1).wait_recv()
            spread(ix - t, t, 2 * t - 1, True, False)

        @pl.when(ix + t < nx)
        def _(t=t):
            down(ix + t, t - 1).wait_recv()
            spread(ix + t, t, 2 * t, False, True)

        if t == 1:
            relay(ix, 0)
        else:

            @pl.when(ix >= t - 1)
            def _(t=t):
                relay(ix - t + 1, 2 * t - 3)

            @pl.when(ix + t - 1 < nx)
            def _(t=t):
                relay(ix + t - 1, 2 * t - 2)

    if nx == 1:
        relay(ix, 0)
    else:

        @pl.when(ix >= nx - 1)
        def _():
            relay(ix - nx + 1, 2 * nx - 3)

        @pl.when(ix + nx - 1 < nx)
        def _():
            relay(ix + nx - 1, 2 * nx - 2)

    def finish(j, slot):
        over(j, slot).wait_send()
        side(j, slot).wait_send()
        side_far(j, slot).wait_send()
        remote(region(j, near), region(j, near), cs.at[slot], cr.at[slot], (ix, iy, near)).wait_recv()
        remote(region(j, far_near), region(j, far_near), qs.at[slot], qr.at[slot], (ix, iy, near)).wait_recv()

    finish(ix, 0)
    for t in range(1, nx):

        @pl.when(ix >= t)
        def _(t=t):
            finish(ix - t, 2 * t - 1)

        @pl.when(ix + t < nx)
        def _(t=t):
            finish(ix + t, 2 * t)

    for t in range(nx - 1):

        @pl.when((ix >= t) & (ix + 1 < nx))
        def _(t=t):
            up(ix - t, t).wait_send()

        @pl.when((ix + t < nx) & (ix >= 1))
        def _(t=t):
            down(ix + t, t).wait_send()

    first.wait_send()
    second.wait_send()


def shards(volume, hat_center, tf_table):
    planes, height, across = volume.shape
    sizes = tuple(lax.axis_size(a) for a in ("gx", "gy", "gz"))
    nx = sizes[0]
    assert sizes[2] == 4 and across == LANES
    extended_rows = -(-(planes + 2) // 16) * 16
    dma = pltpu.SemaphoreType.DMA
    vmem = pl.BlockSpec(memory_space=pltpu.VMEM)
    return pl.pallas_call(
        functools.partial(body, sizes),
        out_shape=jax.ShapeDtypeStruct((4, height, across * nx), F32),
        in_specs=[vmem] * 3,
        out_specs=vmem,
        scratch_shapes=[
            pltpu.VMEM((32, GROUPS * LANES), F32),
            pltpu.VMEM((planes + 2, height + 16, 2 * across), F32),
            pltpu.VMEM((4, planes, height // 2, across), F32),
            pltpu.VMEM((4, planes, height // 4, across), F32),
            pltpu.VMEM((4, planes, height // 4, across), F32),
            pltpu.VMEM((2, height, across), BF16),
            pltpu.VMEM((height, across), BF16),
            pltpu.VMEM((2, height, across), BF16),
            pltpu.VMEM((2, extended_rows, across), BF16),
            pltpu.VMEM((2, 3, extended_rows, across), BF16),
            pltpu.VMEM((4, height, across), F32),
            pltpu.VMEM((4, height // 2, across), F32),
            pltpu.VMEM((4, height // 4, across), F32),
            pltpu.VMEM((4, height // 4, across), F32),
            dma((2,)), dma((2,)),
            dma((2,)), dma((2,)),
            dma((2, 3)), dma((2, 3)),
            dma((2,)), dma((2,)),
            dma((nx,)), dma((nx,)),
            dma((nx,)), dma((nx,)),
            dma((2 * nx,)), dma((2 * nx,)),
            dma((2 * nx,)), dma((2 * nx,)),
            dma((2 * nx,)), dma((2 * nx,)),
        ],
        compiler_params=pltpu.CompilerParams(collective_id=0, has_side_effects=True, vmem_limit_bytes=48 << 20),
    )(volume, hat_center.reshape(1, -1), tf_table)


def solution(mesh):
    in_specs = (P("gz", "gy", "gx"), P(), P())
    out_specs = P(None, "gy", None)
    return jax.shard_map(shards, mesh=mesh, in_specs=in_specs, out_specs=out_specs, check_vma=False)
```

```python
import functools

import jax
import jax.numpy as jnp
from jax import lax
from jax.experimental import pallas as pl
from jax.experimental.pallas import tpu as pltpu
from jax.sharding import PartitionSpec as P

NBIN = 256
HW = 4

ambient = 0.3
grad_floor = 0.01
depth_scale = 1.5

LANES = 128
GROUPS = 7
MESH = pl.DeviceIdType.MESH
F32 = jnp.float32
BF16 = jnp.bfloat16


def build_tables(center_ref, table_ref, tab):
    centers = center_ref[...].astype(F32)
    wide = table_ref[...].astype(F32)
    copies = jnp.concatenate(
        [jnp.broadcast_to(wide[c : c + 1], (8, NBIN)) for c in range(4)], axis=0
    ).astype(BF16)
    centers = jnp.broadcast_to(centers, (LANES, NBIN))
    row = lax.broadcasted_iota(jnp.int32, (LANES, NBIN), 0).astype(F32)
    away = centers - row

    def hats(level):
        return jnp.maximum(0.0, 1.0 - jnp.abs(level - centers) / HW)

    groups = [
        hats((row + LANES) * (1.0 / (2 * LANES)) * (NBIN - 1)),
        jnp.where(away == -3.0, 0.0, jnp.maximum(0.0, 1.0 - jnp.abs(away) / HW)),
        jnp.where((away == 1.0) | (away == 2.0), 1.0, jnp.where((away == 0.0) | (away == -1.0), -1.0, 0.0)),
        jnp.where(away == 3.0, 1.0, jnp.where(away == -2.0, -1.0, 0.0)),
        jnp.where(away == 4.0, 1.0, 0.0),
        jnp.where(away == -3.0, 1.0, 0.0),
        hats(jnp.full((LANES, NBIN), float(NBIN - 1), F32)),
    ]
    for group, weights in enumerate(groups):
        tab[:, group * LANES : (group + 1) * LANES] = lax.dot_general(
            copies, weights.astype(BF16), (((1,), (1,)), ((), ())), preferred_element_type=F32
        )


def lookup(values, tab):
    level = values * float(NBIN - 1)
    bin_index = level.astype(jnp.int32)
    part_bin = level - bin_index.astype(F32)
    quarter = part_bin * 0.25
    coarse = (quarter + 1.5 * 2.0**15) - 1.5 * 2.0**15
    fine = (quarter + 1.5 * 2.0**14) - 1.5 * 2.0**14
    rising = quarter.astype(BF16).astype(F32)
    falling = ((1.0 - part_bin) * 0.25).astype(BF16).astype(F32)
    low_index = bin_index & (LANES - 1)
    high_index = (values * float(2 * LANES)).astype(jnp.int32) & (LANES - 1)
    upper, top = values >= 0.5, values >= 1.0

    def entry(c, group):
        return tab[8 * c : 8 * c + 8, group * LANES : (group + 1) * LANES]

    out = []
    for c in range(4):
        flat, per_coarse, per_fine, per_rising, per_falling = (
            jnp.take_along_axis(entry(c, 1 + k), low_index, axis=1) for k in range(5)
        )
        total = (flat + coarse * per_coarse) + (fine * per_fine + rising * per_rising + falling * per_falling)
        out.append(total)
    for c in range(4):
        high = jnp.take_along_axis(entry(c, 0), high_index, axis=1)
        out[c] = jnp.where(top, entry(c, 6), jnp.where(upper, high, out[c]))
    return out


def body(sizes, vol, center_ref, table_ref, out, tab, xsd, look_a, look_b, look_c, zhalo, face, faces, rows_out, rows_in, part, recv1, recv2, pair,
         zs, zr, fs, fr, rs, rr, es, er, us, ur, ds, dr, ys, yr, cs, cr, qs, qr):
    nx, ny, nz = sizes
    planes, height, across = vol.shape
    ix, iy, iz = lax.axis_index("gx"), lax.axis_index("gy"), lax.axis_index("gz")
    depth = planes * nz

    def at(x, y, z):
        return (x, y, z)

    relations = []
    for s in (-1, 1):
        relations.append((((ix + s >= 0) & (ix + s < nx)), (ix + s, iy, iz)))
        relations.append((((iz + s >= 0) & (iz + s < nz)), (ix, iy, iz + s)))
    for s in (-1, 1):
        for t in (-1, 0, 1):
            relations.append(
                ((iy + s >= 0) & (iy + s < ny) & (ix + t >= 0) & (ix + t < nx), (ix + t, iy + s, iz))
            )
    bit0, bit1 = iz % 2, iz // 2
    near = iz + 1 - 2 * bit0
    far = iz + 2 - 4 * bit1
    faces[...] = jnp.zeros_like(faces)
    rows_in[...] = jnp.zeros_like(rows_in)
    barrier = pltpu.get_barrier_semaphore()
    count = 2
    for there, where in relations:
        count = count + there.astype(jnp.int32)

        @pl.when(there)
        def _(where=where):
            pl.semaphore_signal(barrier, inc=1, device_id=where, device_id_type=MESH)

    for where in ((ix, iy, near), (ix, iy, far)):
        pl.semaphore_signal(barrier, inc=1, device_id=where, device_id_type=MESH)
    pl.semaphore_wait(barrier, count)

    def remote(src, dst, ssem, rsem, where):
        return pltpu.make_async_remote_copy(
            src_ref=src, dst_ref=dst, send_sem=ssem, recv_sem=rsem, device_id=where, device_id_type=MESH
        )

    front, back = iz > 0, iz < nz - 1
    to_back = remote(vol.at[planes - 1], zhalo.at[0], zs.at[0], zr.at[0], (ix, iy, iz + 1))
    to_front = remote(vol.at[0], zhalo.at[1], zs.at[1], zr.at[1], (ix, iy, iz - 1))

    @pl.when(back)
    def _():
        to_back.start()

    @pl.when(front)
    def _():
        to_front.start()

    build_tables(center_ref, table_ref, tab)

    source = lax.broadcasted_iota(jnp.int32, (across, across), 0)
    target = lax.broadcasted_iota(jnp.int32, (across, across), 1)
    gap = source - target
    blur = jnp.where(gap == 0, 2.0, jnp.where(jnp.abs(gap) == 1, 1.0, 0.0))
    slope = jnp.where(gap == 1, 1.0, jnp.where(gap == -1, -1.0, 0.0))
    stencil = jnp.concatenate([blur, slope], axis=1).astype(BF16)

    def edge_columns(cells, plane):
        right = jnp.where((source == across - 1) & (target == 2 * plane + 1), 1.0, 0.0)
        left = jnp.where((source == 0) & (target == 2 * plane), 1.0, 0.0)
        return jnp.dot(cells, (right + left).astype(BF16), preferred_element_type=F32)

    def own_plane(z, acc):
        cells = vol[z]
        xsd[z + 1, pl.ds(8, height), :] = jnp.dot(cells, stencil, preferred_element_type=F32)
        return acc + edge_columns(cells, z + 1)

    columns = lax.fori_loop(0, planes, own_plane, jnp.zeros((height, across), F32))

    @pl.when(back)
    def _():
        to_back.wait_send()
        to_front.wait_recv()

    @pl.when(front)
    def _():
        to_front.wait_send()
        to_back.wait_recv()

    @pl.when(jnp.logical_not(front))
    def _():
        zhalo[0] = jnp.zeros_like(zhalo[0])

    @pl.when(jnp.logical_not(back))
    def _():
        zhalo[1] = jnp.zeros_like(zhalo[1])

    for slot, plane in ((0, 0), (1, planes + 1)):
        cells = zhalo[slot]
        xsd[plane, pl.ds(8, height), :] = jnp.dot(cells, stencil, preferred_element_type=F32)
        columns = columns + edge_columns(cells, plane)
    face[...] = columns.astype(BF16)

    def edge_rows(row):
        own = vol[:, row, :].astype(F32)
        pad = jnp.zeros((rows_out.shape[1] - planes - 2, across), F32)
        ends = [zhalo[slot, row : row + 1, :].astype(F32) for slot in (0, 1)]
        return jnp.concatenate([ends[0], own, ends[1], pad], axis=0).astype(BF16)

    rows_out[0] = edge_rows(0)
    rows_out[1] = edge_rows(height - 1)

    halo = []
    for s, slot in ((1, 0), (-1, 1)):
        sending = (ix + s >= 0) & (ix + s < nx)
        taking = (ix - s >= 0) & (ix - s < nx)
        halo.append((sending, taking, remote(face, faces.at[slot], fs.at[slot], fr.at[slot], (ix + s, iy, iz))))
    for s, side in ((1, 0), (-1, 1)):
        for t in (-1, 0, 1):
            slot = 1 - t
            sending = (iy + s >= 0) & (iy + s < ny) & (ix + t >= 0) & (ix + t < nx)
            taking = (iy - s >= 0) & (iy - s < ny) & (ix - t >= 0) & (ix - t < nx)
            halo.append(
                (sending, taking, remote(rows_out.at[1 - side], rows_in.at[side, slot], rs.at[side, slot], rr.at[side, slot], (ix + t, iy + s, iz)))
            )
    for sending, _, copy in halo:

        @pl.when(sending)
        def _(copy=copy):
            copy.start()

    half, band = height // 2, height // 4
    keep, give = bit0 * half, (1 - bit0) * half
    keep2, give2 = bit1 * band, (1 - bit1) * band

    def look_rows(table, z, start, count):
        cells = vol[z, pl.ds(pl.multiple_of(start, 16), count), :].astype(F32)
        for k in range(count // 8):
            four = lookup(cells[8 * k : 8 * k + 8], tab)
            for c in range(4):
                table[c, z, 8 * k : 8 * k + 8, :] = four[c]

    def look_give(z, carry):
        look_rows(look_a, z, give, half)
        return carry

    lax.fori_loop(0, planes, look_give, 0)

    for sending, taking, copy in halo:

        @pl.when(taking)
        def _(copy=copy):
            copy.wait_recv()

        @pl.when(sending)
        def _(copy=copy):
            copy.wait_send()

    lane = lax.broadcasted_iota(jnp.int32, (height, across), 1)
    both = jnp.where(lane % 2 == 1, faces[0].astype(F32), faces[1].astype(F32))
    ends = jnp.where((lane == 0) | (lane == across - 1), 1.0, 0.0)
    sign = jnp.where(lane == 0, -1.0, jnp.where(lane == across - 1, 1.0, 0.0))

    def add_columns(z, carry):
        placed = pltpu.roll(both, across - 2 * z - 1, 1)
        xsd[z, pl.ds(8, height), :] += jnp.concatenate([placed * ends, placed * sign], axis=1)
        return carry

    lax.fori_loop(0, planes + 2, add_columns, 0)
    count_rows = rows_out.shape[1]
    for side in (0, 1):
        strip = jnp.dot(rows_in[side, 1], stencil, preferred_element_type=F32)
        left = pltpu.roll(rows_in[side, 0].astype(F32), 1, 1)
        right = pltpu.roll(rows_in[side, 2].astype(F32), across - 1, 1)
        short = lax.broadcasted_iota(jnp.int32, (count_rows, across), 1)
        left = jnp.where(short == 0, left, 0.0)
        right = jnp.where(short == across - 1, right, 0.0)
        strip = strip + jnp.concatenate([left + right, right - left], axis=1)
        row = 7 if side == 0 else 8 + height
        for z in range(planes + 2):
            xsd[z, row : row + 1, :] = strip[z : z + 1]

    shade_scale = (1.0 - ambient) / (32.0 * 3.0**0.5)

    sub = lax.broadcasted_iota(jnp.int32, (8, 2 * across), 0)

    def march(row, table, own):
        def gradients(z):
            above = xsd[z, pl.ds(row, 8), :]
            mid = xsd[z, pl.ds(row + 8, 8), :]
            below = xsd[z, pl.ds(row + 16, 8), :]
            up = pltpu.roll(jnp.where(sub == 7, above, mid), 1, 0)
            down = pltpu.roll(jnp.where(sub == 0, below, mid), 7, 0)
            smoothed = up + 2.0 * mid + down
            return smoothed[:, across:], down[:, :across] - up[:, :across], smoothed[:, :across]

        through = jnp.ones((8, across), F32)
        sums = [jnp.zeros((8, across), F32) for _ in range(3)]
        before, here = gradients(0), gradients(1)
        for z in range(planes):
            after = gradients(z + 2)
            grad_x = before[0] + 2.0 * here[0] + after[0]
            grad_y = before[1] + 2.0 * here[1] + after[1]
            grad_z = after[2] - before[2]
            before, here = here, after
            square = (grad_x * grad_x + grad_y * grad_y + grad_z * grad_z) * (1.0 / 1024.0) + grad_floor
            shade = ambient + shade_scale * jnp.abs(grad_x + grad_y + grad_z) * lax.rsqrt(square)
            clear = jnp.exp(table[3, z, pl.ds(own, 8), :] * (-depth_scale / depth))
            weight = through * (1.0 - clear) * shade
            for c in range(3):
                sums[c] = sums[c] + weight * table[c, z, pl.ds(own, 8), :]
            through = through * clear
        for c in range(3):
            part[c, pl.ds(row, 8), :] = sums[c]
        part[3, pl.ds(row, 8), :] = through

    def march_rows(start, table, count, along=None):
        def step(n, carry):
            march(pl.multiple_of(start + 8 * n, 8), table, pl.multiple_of(8 * n, 8))
            if along is not None:
                along(n)
            return carry

        lax.fori_loop(0, count // 8, step, 0)

    share = planes // (half // 8)

    def look_give2(n):
        for k in range(share):
            look_rows(look_b, share * n + k, keep + give2, band)

    march_rows(give, look_a, half, look_give2)
    first = remote(part.at[:, pl.ds(pl.multiple_of(give, half), half), :], recv1, es.at[0], er.at[0], (ix, iy, near))
    first.start()
    march_rows(keep + give2, look_b, band)
    first.wait_recv()

    def fold(mine, theirs, i_am_front):
        ahead = jnp.where(i_am_front, mine[3], theirs[3])
        mixed = []
        for c in range(3):
            a = jnp.where(i_am_front, mine[c], theirs[c])
            b = jnp.where(i_am_front, theirs[c], mine[c])
            mixed.append(a + ahead * b)
        mixed.append(mine[3] * theirs[3])
        return mixed

    def pair_of(start):
        own = pl.ds(pl.multiple_of(keep + start, band), band)
        other = pl.ds(pl.multiple_of(start, band), band)
        return fold([part[c, own, :] for c in range(4)], [recv1[c, other, :] for c in range(4)], bit0 == 0)

    for c, value in enumerate(pair_of(give2)):
        pair[c] = value
    second = remote(pair, recv2, es.at[1], er.at[1], (ix, iy, far))
    second.start()

    def look_keep2(n, carry):
        for k in range(2):
            look_rows(look_c, 2 * n + k, keep + keep2, band)
        return carry

    lax.fori_loop(0, planes // 2, look_keep2, 0)
    march_rows(keep + keep2, look_c, band)
    mine = pair_of(keep2)
    second.wait_recv()
    quad = fold(mine, [recv2[c] for c in range(4)], bit1 == 0)
    quad[3] = 1.0 - quad[3]

    def region(j, z, h):
        b = (z % 2) * 2 + z // 2
        return out.at[2 * h : 2 * h + 2, pl.ds(pl.multiple_of(b * band, band), band), pl.ds(pl.multiple_of(j * across, across), across)]

    for c in range(4):
        region(ix, iz, c // 2)[c % 2] = quad[c]

    def up(j, t, h):
        return remote(region(j, iz, h), region(j, iz, h), us.at[t, h], ur.at[t, h], (ix + 1, iy, iz))

    def down(j, t, h):
        return remote(region(j, iz, h), region(j, iz, h), ds.at[t, h], dr.at[t, h], (ix - 1, iy, iz))

    def over(j, slot, h):
        return remote(region(j, iz, h), region(j, iz, h), ys.at[slot, h], yr.at[slot, h], (ix, iy, far))

    def side(j, slot, h):
        return remote(region(j, iz, h), region(j, iz, h), cs.at[slot, h], cr.at[slot, h], (ix, iy, near))

    def side_far(j, slot, h):
        return remote(region(j, far, h), region(j, far, h), qs.at[slot, h], qr.at[slot, h], (ix, iy, near))

    def take_over(j, slot, h):
        return remote(region(j, far, h), region(j, far, h), ys.at[slot, h], yr.at[slot, h], (ix, iy, far))

    far_near = near + 2 - 4 * bit1

    def spread(j, t, slot, h, upward, downward):
        if upward and t < nx - 1:

            @pl.when(ix + 1 < nx)
            def _():
                up(j, t, h).start()

        if downward and t < nx - 1:

            @pl.when(ix >= 1)
            def _():
                down(j, t, h).start()

        over(j, slot, h).start()
        side(j, slot, h).start()

    def relay(j, slot):
        for h in range(2):
            take_over(j, slot, h).wait_recv()
            side_far(j, slot, h).start()

    for h in range(2):
        spread(ix, 0, 0, h, True, True)
    for t in range(1, nx):
        for h in range(2):

            @pl.when(ix >= t)
            def _(t=t, h=h):
                up(ix - t, t - 1, h).wait_recv()
                spread(ix - t, t, 2 * t - 1, h, True, False)

            @pl.when(ix + t < nx)
            def _(t=t, h=h):
                down(ix + t, t - 1, h).wait_recv()
                spread(ix + t, t, 2 * t, h, False, True)

        if t == 1:
            relay(ix, 0)
        else:

            @pl.when(ix >= t - 1)
            def _(t=t):
                relay(ix - t + 1, 2 * t - 3)

            @pl.when(ix + t - 1 < nx)
            def _(t=t):
                relay(ix + t - 1, 2 * t - 2)

    if nx == 1:
        relay(ix, 0)
    else:

        @pl.when(ix >= nx - 1)
        def _():
            relay(ix - nx + 1, 2 * nx - 3)

        @pl.when(ix + nx - 1 < nx)
        def _():
            relay(ix + nx - 1, 2 * nx - 2)

    def finish(j, slot):
        for h in range(2):
            over(j, slot, h).wait_send()
            side(j, slot, h).wait_send()
            side_far(j, slot, h).wait_send()
            ours, others = region(j, near, h), region(j, far_near, h)
            remote(ours, ours, cs.at[slot, h], cr.at[slot, h], (ix, iy, near)).wait_recv()
            remote(others, others, qs.at[slot, h], qr.at[slot, h], (ix, iy, near)).wait_recv()

    finish(ix, 0)
    for t in range(1, nx):

        @pl.when(ix >= t)
        def _(t=t):
            finish(ix - t, 2 * t - 1)

        @pl.when(ix + t < nx)
        def _(t=t):
            finish(ix + t, 2 * t)

    for t in range(nx - 1):

        @pl.when((ix >= t) & (ix + 1 < nx))
        def _(t=t):
            for h in range(2):
                up(ix - t, t, h).wait_send()

        @pl.when((ix + t < nx) & (ix >= 1))
        def _(t=t):
            for h in range(2):
                down(ix + t, t, h).wait_send()

    first.wait_send()
    second.wait_send()


def shards(volume, hat_center, tf_table):
    planes, height, across = volume.shape
    sizes = tuple(lax.axis_size(a) for a in ("gx", "gy", "gz"))
    nx = sizes[0]
    assert sizes[2] == 4 and across == LANES
    extended_rows = -(-(planes + 2) // 16) * 16
    dma = pltpu.SemaphoreType.DMA
    vmem = pl.BlockSpec(memory_space=pltpu.VMEM)
    return pl.pallas_call(
        functools.partial(body, sizes),
        out_shape=jax.ShapeDtypeStruct((4, height, across * nx), F32),
        in_specs=[vmem] * 3,
        out_specs=vmem,
        scratch_shapes=[
            pltpu.VMEM((32, GROUPS * LANES), F32),
            pltpu.VMEM((planes + 2, height + 16, 2 * across), F32),
            pltpu.VMEM((4, planes, height // 2, across), F32),
            pltpu.VMEM((4, planes, height // 4, across), F32),
            pltpu.VMEM((4, planes, height // 4, across), F32),
            pltpu.VMEM((2, height, across), BF16),
            pltpu.VMEM((height, across), BF16),
            pltpu.VMEM((2, height, across), BF16),
            pltpu.VMEM((2, extended_rows, across), BF16),
            pltpu.VMEM((2, 3, extended_rows, across), BF16),
            pltpu.VMEM((4, height, across), F32),
            pltpu.VMEM((4, height // 2, across), F32),
            pltpu.VMEM((4, height // 4, across), F32),
            pltpu.VMEM((4, height // 4, across), F32),
            dma((2,)), dma((2,)),
            dma((2,)), dma((2,)),
            dma((2, 3)), dma((2, 3)),
            dma((2,)), dma((2,)),
            dma((nx, 2)), dma((nx, 2)),
            dma((nx, 2)), dma((nx, 2)),
            dma((2 * nx, 2)), dma((2 * nx, 2)),
            dma((2 * nx, 2)), dma((2 * nx, 2)),
            dma((2 * nx, 2)), dma((2 * nx, 2)),
        ],
        compiler_params=pltpu.CompilerParams(collective_id=0, has_side_effects=True, vmem_limit_bytes=48 << 20),
    )(volume, hat_center.reshape(1, -1), tf_table)


def solution(mesh):
    in_specs = (P("gz", "gy", "gx"), P(), P())
    out_specs = P(None, "gy", None)
    return jax.shard_map(shards, mesh=mesh, in_specs=in_specs, out_specs=out_specs, check_vma=False)
```

```python
import functools

import jax
import jax.numpy as jnp
from jax import lax
from jax.experimental import pallas as pl
from jax.experimental.pallas import tpu as pltpu
from jax.sharding import PartitionSpec as P

NBIN = 256
HW = 4

ambient = 0.3
grad_floor = 0.01
depth_scale = 1.5

LANES = 128
GROUPS = 7
MESH = pl.DeviceIdType.MESH
F32 = jnp.float32
BF16 = jnp.bfloat16


def build_tables(center_ref, table_ref, tab):
    centers = center_ref[...].astype(F32)
    wide = table_ref[...].astype(F32)
    copies = jnp.concatenate(
        [jnp.broadcast_to(wide[c : c + 1], (8, NBIN)) for c in range(4)], axis=0
    ).astype(BF16)
    centers = jnp.broadcast_to(centers, (LANES, NBIN))
    row = lax.broadcasted_iota(jnp.int32, (LANES, NBIN), 0).astype(F32)
    away = centers - row

    def hats(level):
        return jnp.maximum(0.0, 1.0 - jnp.abs(level - centers) / HW)

    groups = [
        hats((row + LANES) * (1.0 / (2 * LANES)) * (NBIN - 1)),
        jnp.where(away == -3.0, 0.0, jnp.maximum(0.0, 1.0 - jnp.abs(away) / HW)),
        jnp.where((away == 1.0) | (away == 2.0), 1.0, jnp.where((away == 0.0) | (away == -1.0), -1.0, 0.0)),
        jnp.where(away == 3.0, 1.0, jnp.where(away == -2.0, -1.0, 0.0)),
        jnp.where(away == 4.0, 1.0, 0.0),
        jnp.where(away == -3.0, 1.0, 0.0),
        hats(jnp.full((LANES, NBIN), float(NBIN - 1), F32)),
    ]
    for group, weights in enumerate(groups):
        tab[:, group * LANES : (group + 1) * LANES] = lax.dot_general(
            copies, weights.astype(BF16), (((1,), (1,)), ((), ())), preferred_element_type=F32
        )


def lookup(values, tab):
    level = values * float(NBIN - 1)
    bin_index = level.astype(jnp.int32)
    part_bin = level - bin_index.astype(F32)
    quarter = part_bin * 0.25
    coarse = (quarter + 1.5 * 2.0**15) - 1.5 * 2.0**15
    fine = (quarter + 1.5 * 2.0**14) - 1.5 * 2.0**14
    rising = quarter.astype(BF16).astype(F32)
    falling = ((1.0 - part_bin) * 0.25).astype(BF16).astype(F32)
    low_index = bin_index & (LANES - 1)
    high_index = (values * float(2 * LANES)).astype(jnp.int32) & (LANES - 1)
    upper, top = values >= 0.5, values >= 1.0

    def entry(c, group):
        return tab[8 * c : 8 * c + 8, group * LANES : (group + 1) * LANES]

    out = []
    for c in range(4):
        flat, per_coarse, per_fine, per_rising, per_falling = (
            jnp.take_along_axis(entry(c, 1 + k), low_index, axis=1) for k in range(5)
        )
        total = (flat + coarse * per_coarse) + (fine * per_fine + rising * per_rising + falling * per_falling)
        out.append(total)
    for c in range(4):
        high = jnp.take_along_axis(entry(c, 0), high_index, axis=1)
        out[c] = jnp.where(top, entry(c, 6), jnp.where(upper, high, out[c]))
    return out


def body(sizes, vol, center_ref, table_ref, out, tab, xsd, look_a, look_b, look_c, zhalo, face, faces, rows_out, rows_in, part, recv1, recv2, pair,
         zs, zr, fs, fr, rs, rr, es, er, us, ur, ds, dr, ys, yr, cs, cr, qs, qr):
    nx, ny, nz = sizes
    planes, height, across = vol.shape
    ix, iy, iz = lax.axis_index("gx"), lax.axis_index("gy"), lax.axis_index("gz")
    depth = planes * nz

    def at(x, y, z):
        return (x, y, z)

    relations = []
    for s in (-1, 1):
        relations.append((((ix + s >= 0) & (ix + s < nx)), (ix + s, iy, iz)))
        relations.append((((iz + s >= 0) & (iz + s < nz)), (ix, iy, iz + s)))
    for s in (-1, 1):
        for t in (-1, 0, 1):
            relations.append(
                ((iy + s >= 0) & (iy + s < ny) & (ix + t >= 0) & (ix + t < nx), (ix + t, iy + s, iz))
            )
    bit0, bit1 = iz % 2, iz // 2
    near = iz + 1 - 2 * bit0
    far = iz + 2 - 4 * bit1
    faces[...] = jnp.zeros_like(faces)
    rows_in[...] = jnp.zeros_like(rows_in)
    barrier = pltpu.get_barrier_semaphore()
    count = 2
    for there, where in relations:
        count = count + there.astype(jnp.int32)

        @pl.when(there)
        def _(where=where):
            pl.semaphore_signal(barrier, inc=1, device_id=where, device_id_type=MESH)

    for where in ((ix, iy, near), (ix, iy, far)):
        pl.semaphore_signal(barrier, inc=1, device_id=where, device_id_type=MESH)
    pl.semaphore_wait(barrier, count)

    def remote(src, dst, ssem, rsem, where):
        return pltpu.make_async_remote_copy(
            src_ref=src, dst_ref=dst, send_sem=ssem, recv_sem=rsem, device_id=where, device_id_type=MESH
        )

    front, back = iz > 0, iz < nz - 1
    to_back = remote(vol.at[planes - 1], zhalo.at[0], zs.at[0], zr.at[0], (ix, iy, iz + 1))
    to_front = remote(vol.at[0], zhalo.at[1], zs.at[1], zr.at[1], (ix, iy, iz - 1))

    @pl.when(back)
    def _():
        to_back.start()

    @pl.when(front)
    def _():
        to_front.start()

    build_tables(center_ref, table_ref, tab)

    source = lax.broadcasted_iota(jnp.int32, (across, across), 0)
    target = lax.broadcasted_iota(jnp.int32, (across, across), 1)
    gap = source - target
    blur = jnp.where(gap == 0, 2.0, jnp.where(jnp.abs(gap) == 1, 1.0, 0.0))
    slope = jnp.where(gap == 1, 1.0, jnp.where(gap == -1, -1.0, 0.0))
    stencil = jnp.concatenate([blur, slope], axis=1).astype(BF16)

    def edge_columns(cells, plane):
        right = jnp.where((source == across - 1) & (target == 2 * plane + 1), 1.0, 0.0)
        left = jnp.where((source == 0) & (target == 2 * plane), 1.0, 0.0)
        return jnp.dot(cells, (right + left).astype(BF16), preferred_element_type=F32)

    def own_plane(z, acc):
        cells = vol[z]
        xsd[z + 1, pl.ds(8, height), :] = jnp.dot(cells, stencil, preferred_element_type=F32)
        return acc + edge_columns(cells, z + 1)

    columns = lax.fori_loop(0, planes, own_plane, jnp.zeros((height, across), F32))

    @pl.when(back)
    def _():
        to_back.wait_send()
        to_front.wait_recv()

    @pl.when(front)
    def _():
        to_front.wait_send()
        to_back.wait_recv()

    @pl.when(jnp.logical_not(front))
    def _():
        zhalo[0] = jnp.zeros_like(zhalo[0])

    @pl.when(jnp.logical_not(back))
    def _():
        zhalo[1] = jnp.zeros_like(zhalo[1])

    for slot, plane in ((0, 0), (1, planes + 1)):
        cells = zhalo[slot]
        xsd[plane, pl.ds(8, height), :] = jnp.dot(cells, stencil, preferred_element_type=F32)
        columns = columns + edge_columns(cells, plane)
    face[...] = columns.astype(BF16)

    def edge_rows(row):
        own = vol[:, row, :].astype(F32)
        pad = jnp.zeros((rows_out.shape[1] - planes - 2, across), F32)
        ends = [zhalo[slot, row : row + 1, :].astype(F32) for slot in (0, 1)]
        return jnp.concatenate([ends[0], own, ends[1], pad], axis=0).astype(BF16)

    rows_out[0] = edge_rows(0)
    rows_out[1] = edge_rows(height - 1)

    halo = []
    for s, slot in ((1, 0), (-1, 1)):
        sending = (ix + s >= 0) & (ix + s < nx)
        taking = (ix - s >= 0) & (ix - s < nx)
        halo.append((sending, taking, remote(face, faces.at[slot], fs.at[slot], fr.at[slot], (ix + s, iy, iz))))
    for s, side in ((1, 0), (-1, 1)):
        for t in (-1, 0, 1):
            slot = 1 - t
            sending = (iy + s >= 0) & (iy + s < ny) & (ix + t >= 0) & (ix + t < nx)
            taking = (iy - s >= 0) & (iy - s < ny) & (ix - t >= 0) & (ix - t < nx)
            halo.append(
                (sending, taking, remote(rows_out.at[1 - side], rows_in.at[side, slot], rs.at[side, slot], rr.at[side, slot], (ix + t, iy + s, iz)))
            )
    for sending, _, copy in halo:

        @pl.when(sending)
        def _(copy=copy):
            copy.start()

    half, band = height // 2, height // 4
    keep, give = bit0 * half, (1 - bit0) * half
    keep2, give2 = bit1 * band, (1 - bit1) * band

    def look_rows(table, z, start, count):
        cells = vol[z, pl.ds(pl.multiple_of(start, 16), count), :].astype(F32)
        for k in range(count // 8):
            four = lookup(cells[8 * k : 8 * k + 8], tab)
            for c in range(4):
                table[c, z, 8 * k : 8 * k + 8, :] = four[c]

    def look_give(z, carry):
        look_rows(look_a, z, give, half)
        return carry

    lax.fori_loop(0, planes, look_give, 0)

    for sending, taking, copy in halo:

        @pl.when(taking)
        def _(copy=copy):
            copy.wait_recv()

        @pl.when(sending)
        def _(copy=copy):
            copy.wait_send()

    lane = lax.broadcasted_iota(jnp.int32, (height, across), 1)
    both = jnp.where(lane % 2 == 1, faces[0].astype(F32), faces[1].astype(F32))
    ends = jnp.where((lane == 0) | (lane == across - 1), 1.0, 0.0)
    sign = jnp.where(lane == 0, -1.0, jnp.where(lane == across - 1, 1.0, 0.0))

    def add_columns(z, carry):
        placed = pltpu.roll(both, across - 2 * z - 1, 1)
        xsd[z, pl.ds(8, height), :] += jnp.concatenate([placed * ends, placed * sign], axis=1)
        return carry

    lax.fori_loop(0, planes + 2, add_columns, 0)
    count_rows = rows_out.shape[1]
    for side in (0, 1):
        strip = jnp.dot(rows_in[side, 1], stencil, preferred_element_type=F32)
        left = pltpu.roll(rows_in[side, 0].astype(F32), 1, 1)
        right = pltpu.roll(rows_in[side, 2].astype(F32), across - 1, 1)
        short = lax.broadcasted_iota(jnp.int32, (count_rows, across), 1)
        left = jnp.where(short == 0, left, 0.0)
        right = jnp.where(short == across - 1, right, 0.0)
        strip = strip + jnp.concatenate([left + right, right - left], axis=1)
        row = 7 if side == 0 else 8 + height
        for z in range(planes + 2):
            xsd[z, row : row + 1, :] = strip[z : z + 1]

    shade_scale = (1.0 - ambient) / (32.0 * 3.0**0.5)

    sub = lax.broadcasted_iota(jnp.int32, (8, 2 * across), 0)

    def march(row, table, own):
        def gradients(z):
            above = xsd[z, pl.ds(row, 8), :]
            mid = xsd[z, pl.ds(row + 8, 8), :]
            below = xsd[z, pl.ds(row + 16, 8), :]
            up = pltpu.roll(jnp.where(sub == 7, above, mid), 1, 0)
            down = pltpu.roll(jnp.where(sub == 0, below, mid), 7, 0)
            smoothed = up + 2.0 * mid + down
            return smoothed[:, across:], down[:, :across] - up[:, :across], smoothed[:, :across]

        through = jnp.ones((8, across), F32)
        sums = [jnp.zeros((8, across), F32) for _ in range(3)]
        before, here = gradients(0), gradients(1)
        for z in range(planes):
            after = gradients(z + 2)
            grad_x = before[0] + 2.0 * here[0] + after[0]
            grad_y = before[1] + 2.0 * here[1] + after[1]
            grad_z = after[2] - before[2]
            before, here = here, after
            square = (grad_x * grad_x + grad_y * grad_y + grad_z * grad_z) * (1.0 / 1024.0) + grad_floor
            shade = ambient + shade_scale * jnp.abs(grad_x + grad_y + grad_z) * lax.rsqrt(square)
            clear = jnp.exp(table[3, z, pl.ds(own, 8), :] * (-depth_scale / depth))
            weight = through * (1.0 - clear) * shade
            for c in range(3):
                sums[c] = sums[c] + weight * table[c, z, pl.ds(own, 8), :]
            through = through * clear
        for c in range(3):
            part[c, pl.ds(row, 8), :] = sums[c]
        part[3, pl.ds(row, 8), :] = through

    def march_rows(start, table, count, along=None):
        def step(n, carry):
            march(pl.multiple_of(start + 8 * n, 8), table, pl.multiple_of(8 * n, 8))
            if along is not None:
                along(n)
            return carry

        lax.fori_loop(0, count // 8, step, 0)

    share = planes // (half // 8)

    def look_give2(n):
        for k in range(share):
            look_rows(look_b, share * n + k, keep + give2, band)

    march_rows(give, look_a, half, look_give2)
    first = remote(part.at[:, pl.ds(pl.multiple_of(give, half), half), :], recv1, es.at[0], er.at[0], (ix, iy, near))
    first.start()

    def look_keep2(n, carry):
        for k in range(2):
            look_rows(look_c, 2 * n + k, keep + keep2, band)
        return carry

    march_rows(keep + give2, look_b, band, lambda n: look_keep2(n, None))
    first.wait_recv()

    def fold(mine, theirs, i_am_front):
        ahead = jnp.where(i_am_front, mine[3], theirs[3])
        mixed = []
        for c in range(3):
            a = jnp.where(i_am_front, mine[c], theirs[c])
            b = jnp.where(i_am_front, theirs[c], mine[c])
            mixed.append(a + ahead * b)
        mixed.append(mine[3] * theirs[3])
        return mixed

    def pair_of(start):
        own = pl.ds(pl.multiple_of(keep + start, band), band)
        other = pl.ds(pl.multiple_of(start, band), band)
        return fold([part[c, own, :] for c in range(4)], [recv1[c, other, :] for c in range(4)], bit0 == 0)

    for c, value in enumerate(pair_of(give2)):
        pair[c] = value
    second = remote(pair, recv2, es.at[1], er.at[1], (ix, iy, far))
    second.start()

    lax.fori_loop(band // 8, planes // 2, look_keep2, 0)
    march_rows(keep + keep2, look_c, band)
    mine = pair_of(keep2)
    second.wait_recv()
    quad = fold(mine, [recv2[c] for c in range(4)], bit1 == 0)
    quad[3] = 1.0 - quad[3]

    def region(j, z, h):
        b = (z % 2) * 2 + z // 2
        return out.at[2 * h : 2 * h + 2, pl.ds(pl.multiple_of(b * band, band), band), pl.ds(pl.multiple_of(j * across, across), across)]

    for c in range(4):
        region(ix, iz, c // 2)[c % 2] = quad[c]

    def up(j, t, h):
        return remote(region(j, iz, h), region(j, iz, h), us.at[t, h], ur.at[t, h], (ix + 1, iy, iz))

    def down(j, t, h):
        return remote(region(j, iz, h), region(j, iz, h), ds.at[t, h], dr.at[t, h], (ix - 1, iy, iz))

    def over(j, slot, h):
        return remote(region(j, iz, h), region(j, iz, h), ys.at[slot, h], yr.at[slot, h], (ix, iy, far))

    def side(j, slot, h):
        return remote(region(j, iz, h), region(j, iz, h), cs.at[slot, h], cr.at[slot, h], (ix, iy, near))

    def side_far(j, slot, h):
        return remote(region(j, far, h), region(j, far, h), qs.at[slot, h], qr.at[slot, h], (ix, iy, near))

    def take_over(j, slot, h):
        return remote(region(j, far, h), region(j, far, h), ys.at[slot, h], yr.at[slot, h], (ix, iy, far))

    far_near = near + 2 - 4 * bit1

    def spread(j, t, slot, h, upward, downward):
        if upward and t < nx - 1:

            @pl.when(ix + 1 < nx)
            def _():
                up(j, t, h).start()

        if downward and t < nx - 1:

            @pl.when(ix >= 1)
            def _():
                down(j, t, h).start()

        over(j, slot, h).start()
        side(j, slot, h).start()

    def relay(j, slot):
        for h in range(2):
            take_over(j, slot, h).wait_recv()
            side_far(j, slot, h).start()

    for h in range(2):
        spread(ix, 0, 0, h, True, True)
    for t in range(1, nx):
        for h in range(2):

            @pl.when(ix >= t)
            def _(t=t, h=h):
                up(ix - t, t - 1, h).wait_recv()
                spread(ix - t, t, 2 * t - 1, h, True, False)

            @pl.when(ix + t < nx)
            def _(t=t, h=h):
                down(ix + t, t - 1, h).wait_recv()
                spread(ix + t, t, 2 * t, h, False, True)

        if t == 1:
            relay(ix, 0)
        else:

            @pl.when(ix >= t - 1)
            def _(t=t):
                relay(ix - t + 1, 2 * t - 3)

            @pl.when(ix + t - 1 < nx)
            def _(t=t):
                relay(ix + t - 1, 2 * t - 2)

    if nx == 1:
        relay(ix, 0)
    else:

        @pl.when(ix >= nx - 1)
        def _():
            relay(ix - nx + 1, 2 * nx - 3)

        @pl.when(ix + nx - 1 < nx)
        def _():
            relay(ix + nx - 1, 2 * nx - 2)

    def finish(j, slot):
        for h in range(2):
            over(j, slot, h).wait_send()
            side(j, slot, h).wait_send()
            side_far(j, slot, h).wait_send()
            ours, others = region(j, near, h), region(j, far_near, h)
            remote(ours, ours, cs.at[slot, h], cr.at[slot, h], (ix, iy, near)).wait_recv()
            remote(others, others, qs.at[slot, h], qr.at[slot, h], (ix, iy, near)).wait_recv()

    finish(ix, 0)
    for t in range(1, nx):

        @pl.when(ix >= t)
        def _(t=t):
            finish(ix - t, 2 * t - 1)

        @pl.when(ix + t < nx)
        def _(t=t):
            finish(ix + t, 2 * t)

    for t in range(nx - 1):

        @pl.when((ix >= t) & (ix + 1 < nx))
        def _(t=t):
            for h in range(2):
                up(ix - t, t, h).wait_send()

        @pl.when((ix + t < nx) & (ix >= 1))
        def _(t=t):
            for h in range(2):
                down(ix + t, t, h).wait_send()

    first.wait_send()
    second.wait_send()


def shards(volume, hat_center, tf_table):
    planes, height, across = volume.shape
    sizes = tuple(lax.axis_size(a) for a in ("gx", "gy", "gz"))
    nx = sizes[0]
    assert sizes[2] == 4 and across == LANES
    extended_rows = -(-(planes + 2) // 16) * 16
    dma = pltpu.SemaphoreType.DMA
    vmem = pl.BlockSpec(memory_space=pltpu.VMEM)
    return pl.pallas_call(
        functools.partial(body, sizes),
        out_shape=jax.ShapeDtypeStruct((4, height, across * nx), F32),
        in_specs=[vmem] * 3,
        out_specs=vmem,
        scratch_shapes=[
            pltpu.VMEM((32, GROUPS * LANES), F32),
            pltpu.VMEM((planes + 2, height + 16, 2 * across), F32),
            pltpu.VMEM((4, planes, height // 2, across), F32),
            pltpu.VMEM((4, planes, height // 4, across), F32),
            pltpu.VMEM((4, planes, height // 4, across), F32),
            pltpu.VMEM((2, height, across), BF16),
            pltpu.VMEM((height, across), BF16),
            pltpu.VMEM((2, height, across), BF16),
            pltpu.VMEM((2, extended_rows, across), BF16),
            pltpu.VMEM((2, 3, extended_rows, across), BF16),
            pltpu.VMEM((4, height, across), F32),
            pltpu.VMEM((4, height // 2, across), F32),
            pltpu.VMEM((4, height // 4, across), F32),
            pltpu.VMEM((4, height // 4, across), F32),
            dma((2,)), dma((2,)),
            dma((2,)), dma((2,)),
            dma((2, 3)), dma((2, 3)),
            dma((2,)), dma((2,)),
            dma((nx, 2)), dma((nx, 2)),
            dma((nx, 2)), dma((nx, 2)),
            dma((2 * nx, 2)), dma((2 * nx, 2)),
            dma((2 * nx, 2)), dma((2 * nx, 2)),
            dma((2 * nx, 2)), dma((2 * nx, 2)),
        ],
        compiler_params=pltpu.CompilerParams(collective_id=0, has_side_effects=True, vmem_limit_bytes=48 << 20),
    )(volume, hat_center.reshape(1, -1), tf_table)


def solution(mesh):
    in_specs = (P("gz", "gy", "gx"), P(), P())
    out_specs = P(None, "gy", None)
    return jax.shard_map(shards, mesh=mesh, in_specs=in_specs, out_specs=out_specs, check_vma=False)
```
